32 devices in a mesh: group: 2 (over x), tp: 16 (over z, y, core).
Axes of the slice: x: 2, y: 2, z: 4, core: 2. Of those that a mesh axis runs over, the one named last changes fastest.
Arguments:
- hidden_states: bfloat16 [16, 2, 8192], P('group'), parts along dimension 0, may hold values from -6 to 6
- qkv_weight: bfloat16 [10240, 8192], P('tp'), may hold values from -0.0625 to 0.0625
- out_weight: bfloat16 [8192, 8192], P('tp'), may hold values from -0.0625 to 0.0625
- cache_pages: bfloat16 [2048, 128, 256], P(('group', 'tp')), parts along dimension 0, may hold values from -6 to 6
- context_lengths: int32 [16], P('group'), parts along dimension 0, may hold values from 1 to 2046, 8184 in all
- new_units: int32 [128], P('group'), parts along dimension 0, may hold values from 0 to 63, as said below
- old_pages: int32 [2048], P('group'), parts along dimension 0, may hold values from 0 to 1023, as said below
Outputs:
- mixed_out: bfloat16 [16, 2, 8192], P('group', None, 'tp'), parts along dimension 0
- cache_out: bfloat16 [2048, 128, 256], P(('group', 'tp')), parts along dimension 0
The draws below stay inside these ranges and needn't reach their ends.
There are 2 independent parts, one for each index of `group`. The reference program is written for one: setup_inputs(seed, part) draws one part's arguments, and reference() takes and returns one part's arrays. A program takes and returns all parts, laid end to end along the dimension named above; an argument that names none is the same for every part. Nothing has to cross between parts.
Inputs may be any that keep to these rules, and one draw needn't show every extreme that they name: `new_units`: A permutation of all request head groups; slot q of the new layout is on device q // 4. `old_pages`: A permutation of all logical pages (page u * 16 + i is page i of unit u); position p is on device p // 64. The pages that one device holds go to exactly 16 devices of the new layout, exactly 4 to each.
All inputs are finite; a program needn't handle non-finite values.
Results may differ from the reference program's by a relative error of at most 0.013.
Values may be sent and summed in bfloat16 or wider, within the bound.
A program may use at most 128 MiB of HBM per device.

```python
import math
import jax
import jax.numpy as jnp
import numpy as np
from jax import lax

D = 8192
HEADS = 64
KVH = 8
HD = 128
GROUP = 8
U_DEV = 4
MAXCTX = 2048
PAGE = 128
PAGES_DEV = 64
CAP = 4
REQ = 8
PAGES = 1024
N_TP = 16


def layout_tables(key):
    unit_total = U_DEV * N_TP
    page_total = PAGES_DEV * N_TP
    per_unit = MAXCTX // PAGE
    capacity = CAP
    new_units = jax.random.permutation(jax.random.fold_in(key, 101), unit_total).astype(jnp.int32)
    offsets = jax.random.permutation(jax.random.fold_in(key, 102), N_TP).astype(jnp.int32)[:PAGES_DEV // capacity]
    first_perm = jax.random.permutation(jax.random.fold_in(key, 103), N_TP).astype(jnp.int32)
    second_perm = jax.random.permutation(jax.random.fold_in(key, 104), N_TP).astype(jnp.int32)
    within = jax.vmap(lambda sub: jax.random.permutation(sub, PAGES_DEV))(jax.random.split(jax.random.fold_in(key, 105), N_TP)).astype(jnp.int32)
    shuffle = jax.vmap(lambda sub: jax.random.permutation(sub, PAGES_DEV))(jax.random.split(jax.random.fold_in(key, 106), N_TP)).astype(jnp.int32)
    new_position = jnp.arange(page_total, dtype=jnp.int32)
    new_device = new_position // PAGES_DEV
    new_slot = new_position % PAGES_DEV
    page_id = new_units[new_position // per_unit] * per_unit + new_position % per_unit
    drawn_rank = within[new_device, new_slot]
    group_index = drawn_rank // capacity
    member = drawn_rank % capacity
    old_device = second_perm[(first_perm[new_device] + offsets[group_index]) % N_TP]
    old_slot = shuffle[old_device, group_index * capacity + member]
    old_position = old_device * PAGES_DEV + old_slot
    old_pages = jnp.zeros((page_total,), jnp.int32).at[old_position].set(page_id)
    return (new_units, old_pages)


def draw_new_units(key, part):
    return layout_tables(key)[0]


def draw_old_pages(key, part):
    return layout_tables(key)[1]


def block_levels(rng, extent, pieces, smallest, high):
    gain = 1.0
    for axis_at, blocks in pieces:
        heights = jax.random.uniform(jax.random.fold_in(jax.random.fold_in(rng, 6), axis_at), (blocks,), jnp.float32, smallest / len(pieces), high / len(pieces))
        gain = gain * jnp.repeat(jnp.exp(heights), extent[axis_at] // blocks).reshape((-1,) + (1,) * (len(extent) - 1 - axis_at))
    return gain


def split_up(number_of, total, most, lean):
    weights = [(1 << 20) // math.isqrt(rank ** lean) + 1 for rank in range(2, number_of + 1)]
    spare, given = total - most - (number_of - 1), [1] * (number_of - 1)
    while spare > 0:
        candidates = [i for i in range(number_of - 1) if given[i] < most]
        pool, left = sum([weights[i] for i in candidates]), spare
        for i in candidates:
            more = min(most - given[i], max(1, left * weights[i] // pool), spare)
            given[i] = given[i] + more
            spare = spare - more
    return np.array([most] + given)


def ragged(stream_key, count, total, most, lean):
    if count == 2:
        one = jax.random.randint(stream_key, (), max(1, total - most), min(most, total - 1) + 1)
        return jnp.stack([one, total - one])
    sizes = jnp.asarray(split_up(count, total, most, lean), jnp.int32)
    couples = (count - 1) // 2
    giver, sink = sizes[1:1 + 2 * couples:2], sizes[2:2 + 2 * couples:2]
    slack = jnp.minimum(giver - 1, most - sink)
    shifted = jax.random.randint(jax.random.fold_in(stream_key, 1), (couples,), 0, 1 << 20) % (slack + 1)
    sizes = sizes.at[1:1 + 2 * couples:2].set(giver - shifted).at[2:2 + 2 * couples:2].set(sink + shifted)
    return sizes[jax.random.permutation(jax.random.fold_in(stream_key, 2), count)]


def normal_values(own_key, extent, width, limit, cuts=(), kind=jnp.bfloat16):
    array = width * jax.random.normal(own_key, extent, jnp.float32)
    if cuts:
        array = array * block_levels(own_key, extent, cuts, -0.22, 0.18)
    return jnp.clip(array, -limit, limit).astype(kind)


def setup_inputs(seed: int = 0, part: int = 0) -> dict:
    splits = jax.random.split(jax.random.key(seed), 8)
    part_splits = jax.random.split(jax.random.fold_in(splits[7], part), 8)
    hidden_states = normal_values(part_splits[0], (REQ, 2, D), 1.0, 6.0)
    qkv_weight = normal_values(splits[1], (KVH * (GROUP + 2) * HD, D), D ** -0.5, 0.0625, ((0, 16),))
    out_weight = normal_values(splits[2], (D, HEADS * HD), (HEADS * HD) ** -0.5, 0.0625, ((0, 16),))
    cache_pages = normal_values(part_splits[3], (PAGES, PAGE, 2 * HD), 1.0, 6.0, ((0, 16),))
    context_lengths = ragged(part_splits[4], REQ, REQ * (MAXCTX - 2) // 2, MAXCTX - 2, 2).astype(jnp.int32)
    new_units = draw_new_units(jax.random.fold_in(jax.random.fold_in(splits[7], part), 71), part)
    old_pages = draw_old_pages(jax.random.fold_in(jax.random.fold_in(splits[7], part), 71), part)
    return {"hidden_states": hidden_states, "qkv_weight": qkv_weight, "out_weight": out_weight, "cache_pages": cache_pages, "context_lengths": context_lengths, "new_units": new_units, "old_pages": old_pages}


rope_base = 10000.0

def rotate_positions(values, positions):
    half_dim = values.shape[-1] // 2
    frequency = rope_base ** (-(jnp.arange(half_dim, dtype=jnp.float32) * 2.0 / values.shape[-1]))
    angles = positions.astype(jnp.float32)[..., None] * frequency
    cosine = jnp.concatenate([jnp.cos(angles), jnp.cos(angles)], axis=-1)
    sine_table = jnp.concatenate([jnp.sin(angles), jnp.sin(angles)], axis=-1)
    turned = jnp.concatenate([-values[..., half_dim:], values[..., :half_dim]], axis=-1)
    return values * cosine + turned * sine_table

def prepare(unit_qkv, base_lengths):
    group_count = HEADS // KVH
    count_units = unit_qkv.shape[0]
    positions = base_lengths[:, None] + jnp.arange(2, dtype=jnp.int32)[None, :]
    widened = unit_qkv.astype(jnp.float32)
    queries = widened[..., :group_count * HD].reshape(count_units, 2, group_count, HD)
    queries = rotate_positions(queries, positions[:, :, None]).astype(jnp.bfloat16)
    new_keys = rotate_positions(widened[..., group_count * HD:(group_count + 1) * HD], positions).astype(jnp.bfloat16)
    new_values = unit_qkv[..., (group_count + 1) * HD:]
    return (queries, new_keys, new_values)

def reference(hidden_states, qkv_weight, out_weight, cache_pages, context_lengths, new_units, old_pages):
    group_count = HEADS // KVH
    unit_rows = (group_count + 2) * HD
    requests = hidden_states.shape[0]
    total_units = requests * KVH
    per_unit = MAXCTX // PAGE
    page_width = cache_pages.shape[2]
    total_pages = old_pages.shape[0]
    score_scale = 1.0 / math.sqrt(HD)
    flat_rows = hidden_states.reshape(requests * 2, D)
    projected = jnp.dot(flat_rows, qkv_weight.T, preferred_element_type=jnp.float32).astype(jnp.bfloat16)
    unit_qkv = projected.reshape(requests, 2, KVH, unit_rows).transpose(0, 2, 1, 3).reshape(total_units, 2, unit_rows)
    unit_lengths = jnp.repeat(context_lengths, KVH)
    queries, new_keys, new_values = prepare(unit_qkv, unit_lengths)
    stored_position = jnp.zeros((total_pages,), jnp.int32).at[old_pages].set(jnp.arange(total_pages, dtype=jnp.int32))
    contexts = cache_pages[stored_position].reshape(total_units, MAXCTX, page_width)

    def one_unit(packed):
        context, unit_query, keys_new, values_new, valid_count = packed
        cached_keys = jnp.concatenate([context[:, :HD], keys_new], axis=0).astype(jnp.float32)
        cached_values = jnp.concatenate([context[:, HD:], values_new], axis=0).astype(jnp.float32)
        scores = jnp.einsum('sgd,td->sgt', unit_query.astype(jnp.float32), cached_keys) * score_scale
        cached = jnp.arange(MAXCTX, dtype=jnp.int32) < valid_count
        recent = jnp.arange(2, dtype=jnp.int32)[None, :] <= jnp.arange(2, dtype=jnp.int32)[:, None]
        visible = jnp.concatenate([jnp.broadcast_to(cached[None, :], (2, MAXCTX)), recent], axis=1)
        weights = jnp.where(visible[:, None, :], jnp.exp(scores), 0.0)
        totals = lax.optimization_barrier(jnp.sum(weights, axis=-1))
        rounded = lax.optimization_barrier(weights.astype(jnp.bfloat16)).astype(jnp.float32)
        weighted = jnp.einsum('sgt,td->sgd', rounded, cached_values)
        return (weighted / totals[..., None]).astype(jnp.bfloat16)
    attended = lax.map(one_unit, (contexts, queries, new_keys, new_values, unit_lengths))
    heads_out = attended.reshape(requests, KVH, 2, group_count * HD).transpose(0, 2, 1, 3).reshape(requests * 2, HEADS * HD)
    mixed_rows = jnp.dot(heads_out, out_weight.T, preferred_element_type=jnp.float32).astype(jnp.bfloat16).reshape(requests, 2, D)
    slot_contexts = contexts[new_units]
    slot_lengths = unit_lengths[new_units]
    fresh_rows = jnp.concatenate([new_keys, new_values], axis=-1)[new_units]
    positions = jnp.arange(MAXCTX, dtype=jnp.int32)[None, :]
    slot_contexts = jnp.where((positions == slot_lengths[:, None])[..., None], fresh_rows[:, 0:1], slot_contexts)
    slot_contexts = jnp.where((positions == slot_lengths[:, None] + 1)[..., None], fresh_rows[:, 1:2], slot_contexts)
    new_cache = slot_contexts.reshape(total_units * per_unit, PAGE, page_width)
    return (mixed_rows, new_cache)
```

```python
import math

import jax
import jax.numpy as jnp
from jax import lax
from jax.experimental import pallas as pl
from jax.experimental.pallas import tpu as pltpu
from jax.sharding import PartitionSpec as P

D = 8192
HEADS = 64
KVH = 8
HD = 128
U_DEV = 4
MAXCTX = 2048
PAGE = 128


rope_base = 10000.0


def rotate_positions(values, positions):
    half_dim = values.shape[-1] // 2
    frequency = rope_base ** (-(jnp.arange(half_dim, dtype=jnp.float32) * 2.0 / values.shape[-1]))
    angles = positions.astype(jnp.float32)[..., None] * frequency
    cosine = jnp.concatenate([jnp.cos(angles), jnp.cos(angles)], axis=-1)
    sine_table = jnp.concatenate([jnp.sin(angles), jnp.sin(angles)], axis=-1)
    turned = jnp.concatenate([-values[..., half_dim:], values[..., :half_dim]], axis=-1)
    return values * cosine + turned * sine_table


def prepare(unit_qkv, base_lengths):
    group_count = HEADS // KVH
    count_units = unit_qkv.shape[0]
    positions = base_lengths[:, None] + jnp.arange(2, dtype=jnp.int32)[None, :]
    widened = unit_qkv.astype(jnp.float32)
    queries = widened[..., : group_count * HD].reshape(count_units, 2, group_count, HD)
    queries = rotate_positions(queries, positions[:, :, None]).astype(jnp.bfloat16)
    new_keys = rotate_positions(
        widened[..., group_count * HD : (group_count + 1) * HD], positions
    ).astype(jnp.bfloat16)
    new_values = unit_qkv[..., (group_count + 1) * HD :]
    return (queries, new_keys, new_values)


def context_terms(context, queries, valid_count):
    score_scale = 1.0 / math.sqrt(HD)
    cached_keys = context[..., :HD]
    cached_values = context[..., HD:]
    scores = (
        jnp.einsum("psgd,ptd->psgt", queries, cached_keys, preferred_element_type=jnp.float32)
        * score_scale
    )
    visible = jnp.arange(context.shape[1], dtype=jnp.int32)[None, :] < valid_count[:, None]
    weights = jnp.where(visible[:, None, None, :], jnp.exp(scores), 0.0)
    totals = jnp.sum(weights, axis=-1)
    weighted = jnp.einsum(
        "psgt,ptd->psgd",
        weights.astype(jnp.bfloat16),
        cached_values,
        preferred_element_type=jnp.float32,
    )
    return (weighted, totals)


def own_terms(queries, new_keys, new_values):
    score_scale = 1.0 / math.sqrt(HD)
    scores = (
        jnp.einsum("usgd,ujd->usgj", queries, new_keys, preferred_element_type=jnp.float32)
        * score_scale
    )
    recent = jnp.arange(2, dtype=jnp.int32)[None, :] <= jnp.arange(2, dtype=jnp.int32)[:, None]
    weights = jnp.where(recent[None, :, None, :], jnp.exp(scores), 0.0)
    totals = jnp.sum(weights, axis=-1)
    weighted = jnp.einsum(
        "usgj,ujd->usgd",
        weights.astype(jnp.bfloat16),
        new_values,
        preferred_element_type=jnp.float32,
    )
    return (weighted, totals)


def plain_body(hidden_states, qkv_weight, out_weight, cache_pages, context_lengths, new_units, old_pages):
    devices = lax.axis_size("tp")
    device = lax.axis_index("tp")
    requests = hidden_states.shape[0]
    rows_dev = qkv_weight.shape[0]
    pages_dev, page_rows, page_width = cache_pages.shape
    group_count = HEADS // KVH
    unit_rows = (group_count + 2) * HD
    per_unit = MAXCTX // PAGE
    unit_slots = U_DEV
    capacity = max(1, pages_dev // devices)
    total_units = new_units.shape[0]
    total_pages = old_pages.shape[0]
    flat_rows = hidden_states.reshape(requests * 2, D)
    partial_qkv = lax.dot_general(
        flat_rows, qkv_weight, (((1,), (1,)), ((), ())), preferred_element_type=jnp.float32
    )
    partial_qkv = partial_qkv.astype(jnp.bfloat16).reshape(requests, 2, rows_dev)
    slot_index = (
        jnp.zeros((total_units,), jnp.int32)
        .at[new_units]
        .set(jnp.arange(total_units, dtype=jnp.int32))
    )
    own_units = lax.dynamic_slice_in_dim(new_units, device * unit_slots, unit_slots)
    own_requests = own_units // KVH
    own_heads = own_units % KVH
    own_lengths = context_lengths[own_requests]
    local_ids = lax.dynamic_slice_in_dim(old_pages, device * pages_dev, pages_dev)
    local_units = local_ids // per_unit
    local_index = local_ids % per_unit
    target_dev = (slot_index[local_units] * per_unit + local_index) // pages_dev
    local_order = jnp.arange(pages_dev, dtype=jnp.int32)
    send_rank = jnp.sum(
        (
            (target_dev[:, None] == target_dev[None, :])
            & (local_order[None, :] < local_order[:, None])
        ).astype(jnp.int32),
        axis=1,
    )
    outgoing = (
        jnp.zeros((devices, capacity, page_rows, page_width), jnp.bfloat16)
        .at[target_dev, send_rank]
        .set(cache_pages)
    )
    arrived = lax.all_to_all(outgoing, "tp", split_axis=0, concat_axis=0, tiled=True)
    stored_position = (
        jnp.zeros((total_pages,), jnp.int32)
        .at[old_pages]
        .set(jnp.arange(total_pages, dtype=jnp.int32))
    )
    wanted = (
        own_units[:, None] * per_unit + jnp.arange(per_unit, dtype=jnp.int32)[None, :]
    ).reshape(pages_dev)
    source_pos = stored_position[wanted]
    source_dev = source_pos // pages_dev
    source_slot = source_pos % pages_dev
    arrival_rank = jnp.sum(
        (
            (source_dev[:, None] == source_dev[None, :])
            & (source_slot[None, :] < source_slot[:, None])
        ).astype(jnp.int32),
        axis=1,
    )
    relaid = arrived[source_dev, arrival_rank]
    contexts = relaid.reshape(unit_slots, MAXCTX, page_width)
    sources_per_head = unit_rows // rows_dev
    request_table = (new_units // KVH).reshape(devices, unit_slots)
    outgoing_rows = partial_qkv[request_table]
    incoming = lax.all_to_all(outgoing_rows, "tp", split_axis=0, concat_axis=0, tiled=True)
    grouped = jnp.moveaxis(incoming.reshape(KVH, sources_per_head, unit_slots, 2, rows_dev), 2, 0)
    chosen = jnp.take_along_axis(grouped, own_heads[:, None, None, None, None], axis=1)[:, 0]
    own_rows = chosen.transpose(0, 2, 1, 3).reshape(unit_slots, 2, unit_rows)
    queries, new_keys, new_values = prepare(own_rows, own_lengths)
    cache_sums, cache_totals = context_terms(contexts, queries, own_lengths)
    own_sums, own_totals = own_terms(queries, new_keys, new_values)
    attended = ((cache_sums + own_sums) / (cache_totals + own_totals)[..., None]).astype(
        jnp.bfloat16
    )
    attended = attended.reshape(unit_slots, 2, group_count * HD)
    all_heads = lax.all_gather(attended, "tp", axis=0, tiled=True)
    logical = (
        all_heads[slot_index]
        .reshape(requests, KVH, 2, group_count * HD)
        .transpose(0, 2, 1, 3)
        .reshape(requests * 2, HEADS * HD)
    )
    mixed_rows = lax.dot_general(
        logical, out_weight, (((1,), (1,)), ((), ())), preferred_element_type=jnp.float32
    )
    mixed_rows = mixed_rows.astype(jnp.bfloat16).reshape(requests, 2, out_weight.shape[0])
    fresh_rows = jnp.concatenate([new_keys, new_values], axis=-1)
    positions = jnp.arange(MAXCTX, dtype=jnp.int32)[None, :]
    contexts = jnp.where(
        (positions == own_lengths[:, None])[..., None], fresh_rows[:, 0:1], contexts
    )
    contexts = jnp.where(
        (positions == own_lengths[:, None] + 1)[..., None], fresh_rows[:, 1:2], contexts
    )
    return (mixed_rows, contexts.reshape(pages_dev, page_rows, page_width))


def index_tables(context_lengths, new_units, old_pages, pages_dev):
    device = lax.axis_index("tp")
    per_unit = MAXCTX // PAGE
    total_units = new_units.shape[0]
    total_pages = old_pages.shape[0]
    capacity = pages_dev // lax.axis_size("tp")
    places = jnp.arange(pages_dev, dtype=jnp.int32)
    slots = jnp.arange(total_units, dtype=jnp.int32)

    def pick(hit, values):
        return jnp.sum(jnp.where(hit, values[None, :], 0), axis=1)

    def ranks(owner, order):
        before = (owner[:, None] == owner[None, :]) & (order[None, :] < order[:, None])
        return jnp.sum(before.astype(jnp.int32), axis=1)

    local_ids = lax.dynamic_slice_in_dim(old_pages, device * pages_dev, pages_dev)
    target_slot = pick((local_ids // per_unit)[:, None] == new_units[None, :], slots)
    target_dev = target_slot // U_DEV
    sent_at = target_dev * capacity + ranks(target_dev, places)
    sent = places[:, None] == sent_at[None, :]
    send_order = pick(sent, places)
    send_ids = pick(sent, local_ids)
    own_units = lax.dynamic_slice_in_dim(new_units, device * U_DEV, U_DEV)
    wanted = (
        own_units[:, None] * per_unit + jnp.arange(per_unit, dtype=jnp.int32)[None, :]
    ).reshape(pages_dev)
    source_pos = pick(
        wanted[:, None] == old_pages[None, :], jnp.arange(total_pages, dtype=jnp.int32)
    )
    source_dev = source_pos // pages_dev
    arrives_at = source_dev * capacity + ranks(source_dev, source_pos)
    arrival_slot = pick(places[:, None] == arrives_at[None, :], places // per_unit)
    slot_of_unit = pick(slots[:, None] == new_units[None, :], slots)
    requests = context_lengths.shape[0]
    send_units = send_ids // per_unit
    send_lengths = pick(
        (send_units // KVH)[:, None] == jnp.arange(requests, dtype=jnp.int32)[None, :],
        context_lengths,
    )
    send_left = send_lengths - (send_ids % per_unit) * PAGE
    send_query = (send_units % KVH) * requests + send_units // KVH
    own_heads, own_requests = own_units % KVH, own_units // KVH
    table = jnp.concatenate(
        [
            send_query, send_left, arrival_slot, slot_of_unit,
            own_heads * requests + own_requests, own_heads, own_requests,
        ]
    )
    return send_order, arrives_at, table


def sort_kernel(order_ref, pages_ref, out_ref, buf, in_sem, out_sem):
    count = buf.shape[0]

    def inward(i):
        return pltpu.make_async_copy(pages_ref.at[order_ref[i]], buf.at[i], in_sem.at[i])

    def outward(i):
        return pltpu.make_async_copy(buf.at[i], out_ref.at[i], out_sem.at[i])

    @pl.loop(0, count)
    def _(i):
        inward(i).start()

    @pl.loop(0, count)
    def _(i):
        inward(i).wait()
        outward(i).start()

    @pl.loop(0, count)
    def _(i):
        outward(i).wait()


def place_kernel(arrives_ref, lengths_ref, arrived_ref, fresh_ref, out_ref, buf, in_sem, out_sem):
    count = buf.shape[0]
    per_unit = MAXCTX // PAGE

    def inward(i):
        return pltpu.make_async_copy(arrived_ref.at[arrives_ref[i]], buf.at[i], in_sem.at[i])

    def outward(i):
        return pltpu.make_async_copy(buf.at[i], out_ref.at[i], out_sem.at[i])

    @pl.loop(0, count)
    def _(i):
        inward(i).start()

    @pl.loop(0, count)
    def _(i):
        inward(i).wait()
        slot = i // per_unit
        for step in range(2):
            position = lengths_ref[slot] + step

            @pl.when(position // PAGE == i % per_unit)
            def _():
                row = position % PAGE
                base = pl.multiple_of((row // 16) * 16, 16)
                tile = buf[i, pl.ds(base, 16), :]
                line = lax.broadcasted_iota(jnp.int32, tile.shape, 0)
                new = jnp.broadcast_to(fresh_ref[slot, step : step + 1, :], tile.shape)
                mixed = jnp.where(line == row - base, new, tile.astype(jnp.float32))
                buf[i, pl.ds(base, 16), :] = mixed.astype(jnp.bfloat16)

        outward(i).start()

    @pl.loop(0, count)
    def _(i):
        outward(i).wait()


NT = (((1,), (1,)), ((), ()))


def layer_kernel(
    devices, capacity,
    table, hidden_ref, cos_ref, sin_ref, qkv_hbm, out_hbm, pages_hbm,
    arrived_hbm, mixed_ref, fresh_ref,
    qkv_w, out_w, pages, rows_all, spread, queries, new_keys, new_values, part_out, part_in, att_all, flat,
    load_sem, page_send, page_recv, row_send, row_recv, part_send, part_recv, att_send, att_recv,
    self_sem,
):
    me = lax.axis_index("tp")
    pages_dev = pages.shape[0]
    rows = hidden_ref.shape[0]
    requests = rows // 2
    units = requests * KVH
    heads = qkv_w.shape[0]
    tiles = out_w.shape[0]
    group_count = HEADS // KVH
    head_rows = group_count + 2
    score_scale = 1.0 / math.sqrt(HD)
    span = requests * 2 * group_count
    at_left, at_arrival, at_slot = pages_dev, 2 * pages_dev, 3 * pages_dev
    at_own = at_slot + units
    at_head, at_request = at_own + U_DEV, at_own + 2 * U_DEV

    def peer(offset):
        return lax.rem(me + offset, devices)

    def sender(offset):
        return lax.rem(me + devices - offset, devices)

    def remote(src, dst, send, recv, offset):
        return pltpu.make_async_remote_copy(
            src_ref=src, dst_ref=dst, send_sem=send, recv_sem=recv,
            device_id={"tp": peer(offset)}, device_id_type=pl.DeviceIdType.MESH,
        )

    def page_copy(rank, offset):
        return remote(
            pages_hbm.at[peer(offset) * capacity + rank], arrived_hbm.at[me * capacity + rank],
            page_send.at[rank, offset], page_recv.at[rank, offset], offset,
        )

    def page_arrival(rank, offset):
        at = sender(offset) * capacity + rank
        return remote(
            pages_hbm.at[at], arrived_hbm.at[at],
            page_send.at[rank, offset], page_recv.at[rank, offset], offset,
        )

    def row_copy(offset, owner):
        return remote(
            rows_all.at[owner], rows_all.at[owner], row_send.at[offset], row_recv.at[offset], offset
        )

    def part_copy(offset, src, dst):
        return remote(
            part_out.at[src], part_in.at[dst], part_send.at[offset], part_recv.at[offset], offset
        )

    def att_copy(offset, owner):
        block = att_all.at[pl.ds(owner * U_DEV, U_DEV)]
        return remote(block, block, att_send.at[offset], att_recv.at[offset], offset)

    def send_pages(rank):
        @pl.loop(1, devices)
        def _(offset):
            page_copy(rank, offset).start()

    barrier = pltpu.get_barrier_semaphore()

    @pl.loop(1, devices)
    def _(offset):
        pl.semaphore_signal(
            barrier, inc=1, device_id={"tp": peer(offset)}, device_id_type=pl.DeviceIdType.MESH
        )

    loads = [
        pltpu.make_async_copy(qkv_hbm.at[pl.ds(c * HD, HD)], qkv_w.at[c], load_sem.at[c])
        for c in range(heads)
    ]
    loads.append(pltpu.make_async_copy(pages_hbm, pages, load_sem.at[heads]))
    loads += [
        pltpu.make_async_copy(
            out_hbm.at[pl.ds(c * HD, HD)], out_w.at[c], load_sem.at[heads + 1 + c]
        )
        for c in range(tiles)
    ]
    for load in loads[: heads + 1]:
        load.start()
    pl.semaphore_wait(barrier, devices - 1)
    send_pages(0)

    for c in range(heads):
        loads[c].wait()
        part = lax.dot_general(
            hidden_ref[...], qkv_w[c], NT, preferred_element_type=jnp.float32
        ).astype(jnp.bfloat16).astype(jnp.float32)
        turned = part * cos_ref[...] + pltpu.roll(part, HD // 2, 1) * sin_ref[...]
        is_value = lax.rem(me * heads + c, head_rows) == head_rows - 1
        rows_all[me, c] = jnp.where(is_value, part, turned).astype(jnp.bfloat16)

    @pl.loop(1, devices)
    def _(offset):
        row_copy(offset, me).start()

    if capacity > 1:
        send_pages(1)
    for load in loads[heads + 1 :]:
        load.start()
    loads[heads].wait()
    own_pages = pltpu.make_async_copy(
        pages.at[pl.ds(me * capacity, capacity)],
        arrived_hbm.at[pl.ds(me * capacity, capacity)],
        self_sem,
    )
    own_pages.start()

    @pl.loop(1, devices)
    def _(offset):
        row_copy(offset, sender(offset)).wait_recv()

    for h in range(KVH):
        for g in range(group_count):
            at = h * head_rows + g
            spread[pl.ds(h * span + g, rows, stride=group_count), :] = rows_all[
                at // heads, at % heads
            ].astype(jnp.float32)
        at = h * head_rows + group_count
        new_keys[h] = rows_all[at // heads, at % heads]
        new_values[h] = rows_all[(at + 1) // heads, (at + 1) % heads]
        for r in range(requests):
            start = h * span + r * 2 * group_count
            queries[h * requests + r] = spread[start : start + 2 * group_count, :].astype(
                jnp.bfloat16
            )

    lane = lax.broadcasted_iota(jnp.int32, (2 * group_count, PAGE), 1)
    strip = PAGE // capacity

    @pl.loop(0, devices)
    def _(target):
        sums = jnp.zeros((2 * group_count, PAGE), jnp.float32)
        for rank in range(capacity):
            query = queries[table[target * capacity + rank]]
            left = table[at_left + target * capacity + rank]
            page = pages[target * capacity + rank]
            scores = lax.dot_general(
                query, page[:, :HD], NT, preferred_element_type=jnp.float32
            ) * score_scale
            weights = jnp.where(lane < left, jnp.exp(scores), 0.0)
            total = jnp.sum(weights, axis=-1, keepdims=True)
            weighted = jnp.dot(
                weights.astype(jnp.bfloat16), page[:, HD:], preferred_element_type=jnp.float32
            )
            part_out[target, rank] = weighted.astype(jnp.bfloat16)
            high = total.astype(jnp.bfloat16).astype(jnp.float32)
            sums = jnp.where(lane == rank * strip, high, sums)
            sums = jnp.where(lane == rank * strip + strip // 2, total - high, sums)
        part_out[target, capacity] = sums.astype(jnp.bfloat16)

    @pl.loop(1, devices)
    def _(offset):
        part_copy(offset, peer(offset), me).start()

    if capacity > 2:
        send_pages(2)
    part_in[me] = part_out[me]

    own_sums, own_totals = [], []
    row = lax.broadcasted_iota(jnp.int32, (2 * group_count, rows), 0)
    col = lax.broadcasted_iota(jnp.int32, (2 * group_count, rows), 1)
    line = lax.broadcasted_iota(jnp.int32, (rows, HD), 0)
    for j in range(U_DEV):
        request = table[at_request + j]
        keys = new_keys[table[at_head + j]]
        values = new_values[table[at_head + j]]
        scores = lax.dot_general(
            queries[table[at_own + j]], keys, NT, preferred_element_type=jnp.float32
        ) * score_scale
        seen = (col // 2 == request) & (col % 2 <= row // group_count)
        weights = jnp.where(seen, jnp.exp(scores), 0.0)
        own_totals.append(jnp.sum(weights, axis=-1, keepdims=True))
        own_sums.append(
            jnp.dot(weights.astype(jnp.bfloat16), values, preferred_element_type=jnp.float32)
        )
        for step in range(2):
            mine = line == request * 2 + step
            for half, kind in ((0, keys), (1, values)):
                fresh_ref[j, step : step + 1, half * HD : (half + 1) * HD] = jnp.sum(
                    jnp.where(mine, kind.astype(jnp.float32), 0.0), axis=0, keepdims=True
                )

    @pl.loop(1, devices)
    def _(offset):
        part_copy(offset, me, sender(offset)).wait_recv()

    def gather_parts(source, carry):
        sums, totals = carry
        tails = part_in[source, capacity].astype(jnp.float32)
        for rank in range(capacity):
            slot = table[at_arrival + source * capacity + rank]
            part = part_in[source, rank].astype(jnp.float32)
            total = jnp.sum(
                jnp.where(lane // strip == rank, tails, 0.0), axis=-1, keepdims=True
            )
            sums = tuple(s + jnp.where(slot == j, part, 0.0) for j, s in enumerate(sums))
            totals = tuple(t + jnp.where(slot == j, total, 0.0) for j, t in enumerate(totals))
        return sums, totals

    sums, totals = lax.fori_loop(0, devices, gather_parts, (tuple(own_sums), tuple(own_totals)))
    for j in range(U_DEV):
        att_all[me * U_DEV + j] = (sums[j] / totals[j]).astype(jnp.bfloat16)

    @pl.loop(1, devices)
    def _(offset):
        att_copy(offset, me).start()

    for rank in range(3, capacity):
        send_pages(rank)

    @pl.loop(1, devices)
    def _(offset):
        att_copy(offset, sender(offset)).wait_recv()

    for r in range(requests):
        for h in range(KVH):
            slot = table[at_slot + r * KVH + h]
            spread[h * span + r * 2 * group_count : h * span + (r + 1) * 2 * group_count, :] = (
                att_all[slot].astype(jnp.float32)
            )
    for h in range(KVH):
        for g in range(group_count):
            at = (h * group_count + g) * HD
            flat[:, at : at + HD] = spread[
                pl.ds(h * span + g, rows, stride=group_count), :
            ].astype(jnp.bfloat16)
    for c in range(tiles):
        loads[heads + 1 + c].wait()
        mixed_ref[:, c * HD : (c + 1) * HD] = lax.dot_general(
            flat[...], out_w[c], NT, preferred_element_type=jnp.float32
        ).astype(jnp.bfloat16)

    own_pages.wait()

    @pl.loop(1, devices)
    def _(offset):
        row_copy(offset, me).wait_send()
        part_copy(offset, peer(offset), me).wait_send()
        att_copy(offset, me).wait_send()
        for rank in range(capacity):
            page_copy(rank, offset).wait_send()
            page_arrival(rank, offset).wait_recv()


def fused_body(hidden_states, qkv_weight, out_weight, cache_pages, context_lengths, new_units, old_pages):
    devices = lax.axis_size("tp")
    requests = hidden_states.shape[0]
    rows = requests * 2
    pages_dev = cache_pages.shape[0]
    capacity = pages_dev // devices
    heads = qkv_weight.shape[0] // HD
    tiles = out_weight.shape[0] // HD
    group_count = HEADS // KVH
    units = new_units.shape[0]
    hbm = pl.BlockSpec(memory_space=pl.ANY)
    vmem = pl.BlockSpec(memory_space=pltpu.VMEM)
    smem = pl.BlockSpec(memory_space=pltpu.SMEM)
    dma = pltpu.SemaphoreType.DMA
    send_order, arrives_at, table = index_tables(
        context_lengths, new_units, old_pages, pages_dev
    )
    positions = (
        context_lengths[:, None] + jnp.arange(2, dtype=jnp.int32)[None, :]
    ).reshape(rows).astype(jnp.float32)
    half = HD // 2
    frequency = rope_base ** (-(jnp.arange(half, dtype=jnp.float32) * 2.0 / HD))
    angles = positions[:, None] * frequency
    cosine, sine = jnp.cos(angles), jnp.sin(angles)
    cosine = jnp.concatenate([cosine, cosine], axis=-1)
    sine = jnp.concatenate([-sine, sine], axis=-1)

    buffers = [
        pltpu.VMEM(cache_pages.shape, jnp.bfloat16), dma((pages_dev,)), dma((pages_dev,)),
    ]
    outgoing = pl.pallas_call(
        sort_kernel,
        out_shape=jax.ShapeDtypeStruct(cache_pages.shape, jnp.bfloat16),
        in_specs=[smem, hbm],
        out_specs=hbm,
        scratch_shapes=buffers,
        name="sort_pages",
    )(send_order, cache_pages)
    tile = (2 * group_count, HD)
    arrived, mixed, fresh = pl.pallas_call(
        lambda *refs: layer_kernel(devices, capacity, *refs),
        out_shape=(
            jax.ShapeDtypeStruct(cache_pages.shape, jnp.bfloat16),
            jax.ShapeDtypeStruct((rows, out_weight.shape[0]), jnp.bfloat16),
            jax.ShapeDtypeStruct((U_DEV, 2, 2 * HD), jnp.float32),
        ),
        in_specs=[smem, vmem, vmem, vmem, hbm, hbm, hbm],
        out_specs=(hbm, vmem, vmem),
        scratch_shapes=[
            pltpu.VMEM((heads, HD, D), jnp.bfloat16),
            pltpu.VMEM((tiles, HD, HEADS * HD), jnp.bfloat16),
            pltpu.VMEM(cache_pages.shape, jnp.bfloat16),
            pltpu.VMEM((devices, heads, rows, HD), jnp.bfloat16),
            pltpu.VMEM((units * 2 * group_count, HD), jnp.float32),
            pltpu.VMEM((units,) + tile, jnp.bfloat16),
            pltpu.VMEM((KVH, rows, HD), jnp.bfloat16),
            pltpu.VMEM((KVH, rows, HD), jnp.bfloat16),
            pltpu.VMEM((devices, capacity + 1) + tile, jnp.bfloat16),
            pltpu.VMEM((devices, capacity + 1) + tile, jnp.bfloat16),
            pltpu.VMEM((units,) + tile, jnp.bfloat16),
            pltpu.VMEM((rows, HEADS * HD), jnp.bfloat16),
            dma((heads + 1 + tiles,)),
            dma((capacity, devices)), dma((capacity, devices)),
            dma((devices,)), dma((devices,)),
            dma((devices,)), dma((devices,)),
            dma((devices,)), dma((devices,)),
            dma(()),
        ],
        compiler_params=pltpu.CompilerParams(
            collective_id=0, has_side_effects=True, vmem_limit_bytes=48 << 20
        ),
        name="layer",
    )(table, hidden_states.reshape(rows, D), cosine, sine, qkv_weight, out_weight, outgoing)
    own_lengths = jnp.take(
        context_lengths,
        lax.dynamic_slice_in_dim(new_units, lax.axis_index("tp") * U_DEV, U_DEV) // KVH,
    )
    placed = pl.pallas_call(
        place_kernel,
        out_shape=jax.ShapeDtypeStruct(cache_pages.shape, jnp.bfloat16),
        in_specs=[smem, smem, hbm, vmem],
        out_specs=hbm,
        scratch_shapes=buffers,
        name="place_pages",
    )(arrives_at, own_lengths, arrived, fresh)
    return (mixed.reshape(requests, 2, out_weight.shape[0]), placed)


def body(hidden_states, qkv_weight, out_weight, cache_pages, context_lengths, new_units, old_pages):
    devices = lax.axis_size("tp")
    whole_heads = qkv_weight.shape[0] % HD == 0 and out_weight.shape[0] % HD == 0
    whole_shares = cache_pages.shape[0] % devices == 0 and hidden_states.shape[0] == KVH
    chosen = fused_body if whole_heads and whole_shares else plain_body
    return chosen(
        hidden_states, qkv_weight, out_weight, cache_pages, context_lengths, new_units, old_pages
    )


def solution(mesh):
    in_specs = (
        P("group", None, None),
        P("tp", None),
        P("tp", None),
        P(("group", "tp"), None, None),
        P("group"),
        P("group"),
        P("group"),
    )
    out_specs = (P("group", None, "tp"), P(("group", "tp"), None, None))
    return jax.shard_map(body, mesh=mesh, in_specs=in_specs, out_specs=out_specs, check_vma=False)
```

```python
import math

import jax
import jax.numpy as jnp
from jax import lax
from jax.experimental import pallas as pl
from jax.experimental.pallas import tpu as pltpu
from jax.sharding import PartitionSpec as P

D = 8192
HEADS = 64
KVH = 8
HD = 128
U_DEV = 4
MAXCTX = 2048
PAGE = 128


rope_base = 10000.0


def rotate_positions(values, positions):
    half_dim = values.shape[-1] // 2
    frequency = rope_base ** (-(jnp.arange(half_dim, dtype=jnp.float32) * 2.0 / values.shape[-1]))
    angles = positions.astype(jnp.float32)[..., None] * frequency
    cosine = jnp.concatenate([jnp.cos(angles), jnp.cos(angles)], axis=-1)
    sine_table = jnp.concatenate([jnp.sin(angles), jnp.sin(angles)], axis=-1)
    turned = jnp.concatenate([-values[..., half_dim:], values[..., :half_dim]], axis=-1)
    return values * cosine + turned * sine_table


def prepare(unit_qkv, base_lengths):
    group_count = HEADS // KVH
    count_units = unit_qkv.shape[0]
    positions = base_lengths[:, None] + jnp.arange(2, dtype=jnp.int32)[None, :]
    widened = unit_qkv.astype(jnp.float32)
    queries = widened[..., : group_count * HD].reshape(count_units, 2, group_count, HD)
    queries = rotate_positions(queries, positions[:, :, None]).astype(jnp.bfloat16)
    new_keys = rotate_positions(
        widened[..., group_count * HD : (group_count + 1) * HD], positions
    ).astype(jnp.bfloat16)
    new_values = unit_qkv[..., (group_count + 1) * HD :]
    return (queries, new_keys, new_values)


def context_terms(context, queries, valid_count):
    score_scale = 1.0 / math.sqrt(HD)
    cached_keys = context[..., :HD]
    cached_values = context[..., HD:]
    scores = (
        jnp.einsum("psgd,ptd->psgt", queries, cached_keys, preferred_element_type=jnp.float32)
        * score_scale
    )
    visible = jnp.arange(context.shape[1], dtype=jnp.int32)[None, :] < valid_count[:, None]
    weights = jnp.where(visible[:, None, None, :], jnp.exp(scores), 0.0)
    totals = jnp.sum(weights, axis=-1)
    weighted = jnp.einsum(
        "psgt,ptd->psgd",
        weights.astype(jnp.bfloat16),
        cached_values,
        preferred_element_type=jnp.float32,
    )
    return (weighted, totals)


def own_terms(queries, new_keys, new_values):
    score_scale = 1.0 / math.sqrt(HD)
    scores = (
        jnp.einsum("usgd,ujd->usgj", queries, new_keys, preferred_element_type=jnp.float32)
        * score_scale
    )
    recent = jnp.arange(2, dtype=jnp.int32)[None, :] <= jnp.arange(2, dtype=jnp.int32)[:, None]
    weights = jnp.where(recent[None, :, None, :], jnp.exp(scores), 0.0)
    totals = jnp.sum(weights, axis=-1)
    weighted = jnp.einsum(
        "usgj,ujd->usgd",
        weights.astype(jnp.bfloat16),
        new_values,
        preferred_element_type=jnp.float32,
    )
    return (weighted, totals)


def plain_body(hidden_states, qkv_weight, out_weight, cache_pages, context_lengths, new_units, old_pages):
    devices = lax.axis_size("tp")
    device = lax.axis_index("tp")
    requests = hidden_states.shape[0]
    rows_dev = qkv_weight.shape[0]
    pages_dev, page_rows, page_width = cache_pages.shape
    group_count = HEADS // KVH
    unit_rows = (group_count + 2) * HD
    per_unit = MAXCTX // PAGE
    unit_slots = U_DEV
    capacity = max(1, pages_dev // devices)
    total_units = new_units.shape[0]
    total_pages = old_pages.shape[0]
    flat_rows = hidden_states.reshape(requests * 2, D)
    partial_qkv = lax.dot_general(
        flat_rows, qkv_weight, (((1,), (1,)), ((), ())), preferred_element_type=jnp.float32
    )
    partial_qkv = partial_qkv.astype(jnp.bfloat16).reshape(requests, 2, rows_dev)
    slot_index = (
        jnp.zeros((total_units,), jnp.int32)
        .at[new_units]
        .set(jnp.arange(total_units, dtype=jnp.int32))
    )
    own_units = lax.dynamic_slice_in_dim(new_units, device * unit_slots, unit_slots)
    own_requests = own_units // KVH
    own_heads = own_units % KVH
    own_lengths = context_lengths[own_requests]
    local_ids = lax.dynamic_slice_in_dim(old_pages, device * pages_dev, pages_dev)
    local_units = local_ids // per_unit
    local_index = local_ids % per_unit
    target_dev = (slot_index[local_units] * per_unit + local_index) // pages_dev
    local_order = jnp.arange(pages_dev, dtype=jnp.int32)
    send_rank = jnp.sum(
        (
            (target_dev[:, None] == target_dev[None, :])
            & (local_order[None, :] < local_order[:, None])
        ).astype(jnp.int32),
        axis=1,
    )
    outgoing = (
        jnp.zeros((devices, capacity, page_rows, page_width), jnp.bfloat16)
        .at[target_dev, send_rank]
        .set(cache_pages)
    )
    arrived = lax.all_to_all(outgoing, "tp", split_axis=0, concat_axis=0, tiled=True)
    stored_position = (
        jnp.zeros((total_pages,), jnp.int32)
        .at[old_pages]
        .set(jnp.arange(total_pages, dtype=jnp.int32))
    )
    wanted = (
        own_units[:, None] * per_unit + jnp.arange(per_unit, dtype=jnp.int32)[None, :]
    ).reshape(pages_dev)
    source_pos = stored_position[wanted]
    source_dev = source_pos // pages_dev
    source_slot = source_pos % pages_dev
    arrival_rank = jnp.sum(
        (
            (source_dev[:, None] == source_dev[None, :])
            & (source_slot[None, :] < source_slot[:, None])
        ).astype(jnp.int32),
        axis=1,
    )
    relaid = arrived[source_dev, arrival_rank]
    contexts = relaid.reshape(unit_slots, MAXCTX, page_width)
    sources_per_head = unit_rows // rows_dev
    request_table = (new_units // KVH).reshape(devices, unit_slots)
    outgoing_rows = partial_qkv[request_table]
    incoming = lax.all_to_all(outgoing_rows, "tp", split_axis=0, concat_axis=0, tiled=True)
    grouped = jnp.moveaxis(incoming.reshape(KVH, sources_per_head, unit_slots, 2, rows_dev), 2, 0)
    chosen = jnp.take_along_axis(grouped, own_heads[:, None, None, None, None], axis=1)[:, 0]
    own_rows = chosen.transpose(0, 2, 1, 3).reshape(unit_slots, 2, unit_rows)
    queries, new_keys, new_values = prepare(own_rows, own_lengths)
    cache_sums, cache_totals = context_terms(contexts, queries, own_lengths)
    own_sums, own_totals = own_terms(queries, new_keys, new_values)
    attended = ((cache_sums + own_sums) / (cache_totals + own_totals)[..., None]).astype(
        jnp.bfloat16
    )
    attended = attended.reshape(unit_slots, 2, group_count * HD)
    all_heads = lax.all_gather(attended, "tp", axis=0, tiled=True)
    logical = (
        all_heads[slot_index]
        .reshape(requests, KVH, 2, group_count * HD)
        .transpose(0, 2, 1, 3)
        .reshape(requests * 2, HEADS * HD)
    )
    mixed_rows = lax.dot_general(
        logical, out_weight, (((1,), (1,)), ((), ())), preferred_element_type=jnp.float32
    )
    mixed_rows = mixed_rows.astype(jnp.bfloat16).reshape(requests, 2, out_weight.shape[0])
    fresh_rows = jnp.concatenate([new_keys, new_values], axis=-1)
    positions = jnp.arange(MAXCTX, dtype=jnp.int32)[None, :]
    contexts = jnp.where(
        (positions == own_lengths[:, None])[..., None], fresh_rows[:, 0:1], contexts
    )
    contexts = jnp.where(
        (positions == own_lengths[:, None] + 1)[..., None], fresh_rows[:, 1:2], contexts
    )
    return (mixed_rows, contexts.reshape(pages_dev, page_rows, page_width))


def index_tables(context_lengths, new_units, old_pages, pages_dev):
    device = lax.axis_index("tp")
    per_unit = MAXCTX // PAGE
    total_units = new_units.shape[0]
    total_pages = old_pages.shape[0]
    capacity = pages_dev // lax.axis_size("tp")
    places = jnp.arange(pages_dev, dtype=jnp.int32)
    slots = jnp.arange(total_units, dtype=jnp.int32)

    def pick(hit, values):
        return jnp.sum(jnp.where(hit, values[None, :], 0), axis=1)

    def ranks(owner, order):
        before = (owner[:, None] == owner[None, :]) & (order[None, :] < order[:, None])
        return jnp.sum(before.astype(jnp.int32), axis=1)

    local_ids = lax.dynamic_slice_in_dim(old_pages, device * pages_dev, pages_dev)
    target_slot = pick((local_ids // per_unit)[:, None] == new_units[None, :], slots)
    target_dev = target_slot // U_DEV
    sent_at = target_dev * capacity + ranks(target_dev, places)
    sent = places[:, None] == sent_at[None, :]
    send_order = pick(sent, places)
    send_ids = pick(sent, local_ids)
    send_slot = pick(sent, target_slot % U_DEV)
    own_units = lax.dynamic_slice_in_dim(new_units, device * U_DEV, U_DEV)
    wanted = (
        own_units[:, None] * per_unit + jnp.arange(per_unit, dtype=jnp.int32)[None, :]
    ).reshape(pages_dev)
    source_pos = pick(
        wanted[:, None] == old_pages[None, :], jnp.arange(total_pages, dtype=jnp.int32)
    )
    source_dev = source_pos // pages_dev
    arrives_at = source_dev * capacity + ranks(source_dev, source_pos)
    slot_of_unit = pick(slots[:, None] == new_units[None, :], slots)
    requests = context_lengths.shape[0]
    send_units = send_ids // per_unit
    send_lengths = pick(
        (send_units // KVH)[:, None] == jnp.arange(requests, dtype=jnp.int32)[None, :],
        context_lengths,
    )
    send_left = send_lengths - (send_ids % per_unit) * PAGE
    send_query = (send_units % KVH) * requests + send_units // KVH
    own_heads, own_requests = own_units % KVH, own_units // KVH
    table = jnp.concatenate(
        [
            send_query, send_left, send_slot, slot_of_unit,
            own_heads * requests + own_requests, own_heads, own_requests,
        ]
    )
    return send_order, arrives_at, table


def sort_kernel(order_ref, pages_ref, out_ref, buf, in_sem, out_sem):
    count = buf.shape[0]

    def inward(i):
        return pltpu.make_async_copy(pages_ref.at[order_ref[i]], buf.at[i], in_sem.at[i])

    def outward(i):
        return pltpu.make_async_copy(buf.at[i], out_ref.at[i], out_sem.at[i])

    @pl.loop(0, count)
    def _(i):
        inward(i).start()

    @pl.loop(0, count)
    def _(i):
        inward(i).wait()
        outward(i).start()

    @pl.loop(0, count)
    def _(i):
        outward(i).wait()


def place_kernel(arrives_ref, lengths_ref, arrived_ref, fresh_ref, out_ref, buf, in_sem, out_sem):
    count = buf.shape[0]
    per_unit = MAXCTX // PAGE

    def inward(i):
        return pltpu.make_async_copy(arrived_ref.at[arrives_ref[i]], buf.at[i], in_sem.at[i])

    def outward(i):
        return pltpu.make_async_copy(buf.at[i], out_ref.at[i], out_sem.at[i])

    @pl.loop(0, count)
    def _(i):
        inward(i).start()

    @pl.loop(0, count)
    def _(i):
        inward(i).wait()
        slot = i // per_unit
        for step in range(2):
            position = lengths_ref[slot] + step

            @pl.when(position // PAGE == i % per_unit)
            def _():
                row = position % PAGE
                base = pl.multiple_of((row // 16) * 16, 16)
                tile = buf[i, pl.ds(base, 16), :]
                line = lax.broadcasted_iota(jnp.int32, tile.shape, 0)
                new = jnp.broadcast_to(fresh_ref[slot, step : step + 1, :], tile.shape)
                mixed = jnp.where(line == row - base, new, tile.astype(jnp.float32))
                buf[i, pl.ds(base, 16), :] = mixed.astype(jnp.bfloat16)

        outward(i).start()

    @pl.loop(0, count)
    def _(i):
        outward(i).wait()


NT = (((1,), (1,)), ((), ()))


def layer_kernel(
    devices, capacity,
    table, hidden_ref, cos_ref, sin_ref, qkv_hbm, out_hbm, pages_hbm,
    arrived_hbm, mixed_ref, fresh_ref,
    qkv_w, out_w, pages, rows_all, spread, queries, new_keys, new_values, part_out, part_in, swap_out, swap_in, att_all, flat,
    load_sem, page_send, page_recv, row_send, row_recv, part_send, part_recv, att_send, att_recv,
    self_sem,
):
    me = lax.axis_index("tp")
    pages_dev = pages.shape[0]
    rows = hidden_ref.shape[0]
    requests = rows // 2
    units = requests * KVH
    heads = qkv_w.shape[0]
    tiles = out_w.shape[0]
    group_count = HEADS // KVH
    head_rows = group_count + 2
    score_scale = 1.0 / math.sqrt(HD)
    span = requests * 2 * group_count
    at_left, at_target, at_slot = pages_dev, 2 * pages_dev, 3 * pages_dev
    at_own = at_slot + units
    at_head, at_request = at_own + U_DEV, at_own + 2 * U_DEV

    half = devices // 2
    here, side = lax.rem(me, half), me // half
    partner = lax.rem(me + half, devices)

    def near(offset):
        return side * half + lax.rem(here + offset, half)

    def near_sender(offset):
        return side * half + lax.rem(here + half - offset, half)

    def far(offset):
        return (1 - side) * half + lax.rem(here + offset, half)

    def far_sender(offset):
        return (1 - side) * half + lax.rem(here + half - offset, half)

    def remote(src, dst, send, recv, device):
        return pltpu.make_async_remote_copy(
            src_ref=src, dst_ref=dst, send_sem=send, recv_sem=recv,
            device_id={"tp": device}, device_id_type=pl.DeviceIdType.MESH,
        )

    def page_copy(rank, place, device):
        return remote(
            pages_hbm.at[device * capacity + rank], arrived_hbm.at[me * capacity + rank],
            page_send.at[rank, place], page_recv.at[rank, place], device,
        )

    def page_arrival(rank, place, device):
        at = device * capacity + rank
        return remote(
            pages_hbm.at[at], arrived_hbm.at[at],
            page_send.at[rank, place], page_recv.at[rank, place], device,
        )

    def row_copy(stage, place, owner, device):
        block = rows_all.at[owner]
        return remote(block, block, row_send.at[stage, place], row_recv.at[stage, place], device)

    def att_copy(stage, place, owner, device):
        block = att_all.at[pl.ds(owner * U_DEV, U_DEV)]
        return remote(block, block, att_send.at[stage, place], att_recv.at[stage, place], device)

    def part_copy(place, src, dst, device):
        return remote(
            part_out.at[src], part_in.at[dst], part_send.at[place], part_recv.at[place], device
        )

    def swap_copy():
        return remote(swap_out, swap_in, part_send.at[0], part_recv.at[0], partner)

    batches = 2 * capacity

    def send_pages(batch):
        if batch >= batches:
            return
        rank, low, high = batch // 2, (batch % 2) * (half // 2), (batch % 2 + 1) * (half // 2)
        if batch % 2:
            high = half

        if low == 0:
            page_copy(rank, 0, partner).start()

        @pl.loop(max(low, 1), high)
        def _(offset):
            page_copy(rank, offset, far(offset)).start()
            page_copy(rank, half + offset, near(offset)).start()

    def pack_totals(values):
        packed = jnp.zeros((2 * group_count, PAGE), jnp.float32)
        for j, total in enumerate(values):
            top = total.astype(jnp.bfloat16).astype(jnp.float32)
            packed = jnp.where(lane == j * strip, top, packed)
            packed = jnp.where(lane == j * strip + strip // 2, total - top, packed)
        return packed.astype(jnp.bfloat16)

    def unpack_total(packed, j):
        return jnp.sum(jnp.where(lane // strip == j, packed, 0.0), axis=-1, keepdims=True)

    lane = lax.broadcasted_iota(jnp.int32, (2 * group_count, PAGE), 1)
    strip = PAGE // U_DEV

    barrier = pltpu.get_barrier_semaphore()

    @pl.loop(1, devices)
    def _(offset):
        pl.semaphore_signal(
            barrier, inc=1, device_id={"tp": lax.rem(me + offset, devices)}, device_id_type=pl.DeviceIdType.MESH
        )

    loads = [
        pltpu.make_async_copy(qkv_hbm.at[pl.ds(c * HD, HD)], qkv_w.at[c], load_sem.at[c])
        for c in range(heads)
    ]
    loads.append(pltpu.make_async_copy(pages_hbm, pages, load_sem.at[heads]))
    loads += [
        pltpu.make_async_copy(
            out_hbm.at[pl.ds(c * HD, HD)], out_w.at[c], load_sem.at[heads + 1 + c]
        )
        for c in range(tiles)
    ]
    for load in loads[: heads + 1]:
        load.start()
    pl.semaphore_wait(barrier, devices - 1)
    send_pages(0)

    for c in range(heads):
        loads[c].wait()
        part = lax.dot_general(
            hidden_ref[...], qkv_w[c], NT, preferred_element_type=jnp.float32
        ).astype(jnp.bfloat16).astype(jnp.float32)
        turned = part * cos_ref[...] + pltpu.roll(part, HD // 2, 1) * sin_ref[...]
        is_value = lax.rem(me * heads + c, head_rows) == head_rows - 1
        rows_all[me, c] = jnp.where(is_value, part, turned).astype(jnp.bfloat16)

    row_copy(0, 0, me, partner).start()

    @pl.loop(1, half)
    def _(offset):
        row_copy(0, offset, me, near(offset)).start()

    send_pages(1)
    for load in loads[heads + 1 :]:
        load.start()
    loads[heads].wait()
    own_pages = pltpu.make_async_copy(
        pages.at[pl.ds(me * capacity, capacity)],
        arrived_hbm.at[pl.ds(me * capacity, capacity)],
        self_sem,
    )
    own_pages.start()

    row_copy(0, 0, partner, partner).wait_recv()

    @pl.loop(1, half)
    def _(offset):
        row_copy(1, offset, partner, near(offset)).start()

    send_pages(2)

    @pl.loop(1, half)
    def _(offset):
        source = near_sender(offset)
        row_copy(0, offset, source, source).wait_recv()
        row_copy(1, offset, lax.rem(source + half, devices), source).wait_recv()

    for h in range(KVH):
        for g in range(group_count):
            at = h * head_rows + g
            spread[pl.ds(h * span + g, rows, stride=group_count), :] = rows_all[
                at // heads, at % heads
            ].astype(jnp.float32)
        at = h * head_rows + group_count
        new_keys[h] = rows_all[at // heads, at % heads]
        new_values[h] = rows_all[(at + 1) // heads, (at + 1) % heads]
        for r in range(requests):
            start = h * span + r * 2 * group_count
            queries[h * requests + r] = spread[start : start + 2 * group_count, :].astype(
                jnp.bfloat16
            )

    @pl.loop(0, devices)
    def _(target):
        zero = jnp.zeros((2 * group_count, PAGE), jnp.float32)
        sums, totals = [zero] * U_DEV, [zero[:, :1]] * U_DEV
        for rank in range(capacity):
            query = queries[table[target * capacity + rank]]
            left = table[at_left + target * capacity + rank]
            page = pages[target * capacity + rank]
            scores = lax.dot_general(
                query, page[:, :HD], NT, preferred_element_type=jnp.float32
            ) * score_scale
            weights = jnp.where(lane < left, jnp.exp(scores), 0.0)
            total = jnp.sum(weights, axis=-1, keepdims=True)
            weighted = jnp.dot(
                weights.astype(jnp.bfloat16), page[:, HD:], preferred_element_type=jnp.float32
            )
            slot = table[at_target + target * capacity + rank]
            for j in range(U_DEV):
                sums[j] = sums[j] + jnp.where(slot == j, weighted, 0.0)
                totals[j] = totals[j] + jnp.where(slot == j, total, 0.0)
        place, which = lax.rem(target, half), target // half
        for j in range(U_DEV):
            part_out[place, which, j] = sums[j].astype(jnp.bfloat16)
        part_out[place, which, U_DEV] = pack_totals(totals)

    @pl.loop(1, half)
    def _(offset):
        part_copy(offset, lax.rem(here + offset, half), here, near(offset)).start()

    send_pages(3)

    own_sums, own_totals = [], []
    row = lax.broadcasted_iota(jnp.int32, (2 * group_count, rows), 0)
    col = lax.broadcasted_iota(jnp.int32, (2 * group_count, rows), 1)
    line = lax.broadcasted_iota(jnp.int32, (rows, HD), 0)
    for j in range(U_DEV):
        request = table[at_request + j]
        keys = new_keys[table[at_head + j]]
        values = new_values[table[at_head + j]]
        scores = lax.dot_general(
            queries[table[at_own + j]], keys, NT, preferred_element_type=jnp.float32
        ) * score_scale
        seen = (col // 2 == request) & (col % 2 <= row // group_count)
        weights = jnp.where(seen, jnp.exp(scores), 0.0)
        own_totals.append(jnp.sum(weights, axis=-1, keepdims=True))
        own_sums.append(
            jnp.dot(weights.astype(jnp.bfloat16), values, preferred_element_type=jnp.float32)
        )
        for step in range(2):
            mine = line == request * 2 + step
            for part, kind in ((0, keys), (1, values)):
                fresh_ref[j, step : step + 1, part * HD : (part + 1) * HD] = jnp.sum(
                    jnp.where(mine, kind.astype(jnp.float32), 0.0), axis=0, keepdims=True
                )

    @pl.loop(1, half)
    def _(offset):
        source = near_sender(offset)
        part_copy(offset, here, lax.rem(here + half - offset, half), source).wait_recv()

    def half_sum(which):
        def add(offset, carry):
            block = part_in.at[lax.rem(here + offset, half), which]
            return tuple(c + block[j].astype(jnp.float32) for j, c in enumerate(carry))

        first = tuple(
            part_out[here, which, j].astype(jnp.float32) for j in range(U_DEV + 1)
        )
        return lax.fori_loop(1, half, add, first)

    away = half_sum(1 - side)
    for j in range(U_DEV):
        swap_out[j] = away[j].astype(jnp.bfloat16)
    swap_out[U_DEV] = pack_totals([unpack_total(away[U_DEV], j) for j in range(U_DEV)])
    kept = half_sum(side)
    swap_copy().start()
    send_pages(4)
    swap_copy().wait_recv()
    packed = kept[U_DEV] + swap_in[U_DEV].astype(jnp.float32)
    for j in range(U_DEV):
        total = own_totals[j] + unpack_total(packed, j)
        weighted = own_sums[j] + kept[j] + swap_in[j].astype(jnp.float32)
        att_all[me * U_DEV + j] = (weighted / total).astype(jnp.bfloat16)

    att_copy(0, 0, me, partner).start()

    @pl.loop(1, half)
    def _(offset):
        att_copy(0, offset, me, near(offset)).start()

    send_pages(5)
    att_copy(0, 0, partner, partner).wait_recv()

    @pl.loop(1, half)
    def _(offset):
        att_copy(1, offset, partner, near(offset)).start()

    for batch in range(6, batches):
        send_pages(batch)

    @pl.loop(1, half)
    def _(offset):
        source = near_sender(offset)
        att_copy(0, offset, source, source).wait_recv()
        att_copy(1, offset, lax.rem(source + half, devices), source).wait_recv()

    for r in range(requests):
        for h in range(KVH):
            slot = table[at_slot + r * KVH + h]
            spread[h * span + r * 2 * group_count : h * span + (r + 1) * 2 * group_count, :] = (
                att_all[slot].astype(jnp.float32)
            )
    for h in range(KVH):
        for g in range(group_count):
            at = (h * group_count + g) * HD
            flat[:, at : at + HD] = spread[
                pl.ds(h * span + g, rows, stride=group_count), :
            ].astype(jnp.bfloat16)
    for c in range(tiles):
        loads[heads + 1 + c].wait()
        mixed_ref[:, c * HD : (c + 1) * HD] = lax.dot_general(
            flat[...], out_w[c], NT, preferred_element_type=jnp.float32
        ).astype(jnp.bfloat16)

    own_pages.wait()

    row_copy(0, 0, me, partner).wait_send()
    att_copy(0, 0, me, partner).wait_send()
    swap_copy().wait_send()

    @pl.loop(1, half)
    def _(offset):
        for stage, owner in ((0, me), (1, partner)):
            row_copy(stage, offset, owner, near(offset)).wait_send()
            att_copy(stage, offset, owner, near(offset)).wait_send()
        part_copy(offset, lax.rem(here + offset, half), here, near(offset)).wait_send()

    for rank in range(capacity):
        page_copy(rank, 0, partner).wait_send()
        page_arrival(rank, 0, partner).wait_recv()

        @pl.loop(1, half)
        def _(offset):
            page_copy(rank, offset, far(offset)).wait_send()
            page_arrival(rank, offset, far_sender(offset)).wait_recv()
            page_copy(rank, half + offset, near(offset)).wait_send()
            page_arrival(rank, half + offset, near_sender(offset)).wait_recv()


def fused_body(hidden_states, qkv_weight, out_weight, cache_pages, context_lengths, new_units, old_pages):
    devices = lax.axis_size("tp")
    requests = hidden_states.shape[0]
    rows = requests * 2
    pages_dev = cache_pages.shape[0]
    capacity = pages_dev // devices
    heads = qkv_weight.shape[0] // HD
    tiles = out_weight.shape[0] // HD
    group_count = HEADS // KVH
    units = new_units.shape[0]
    hbm = pl.BlockSpec(memory_space=pl.ANY)
    vmem = pl.BlockSpec(memory_space=pltpu.VMEM)
    smem = pl.BlockSpec(memory_space=pltpu.SMEM)
    dma = pltpu.SemaphoreType.DMA
    send_order, arrives_at, table = index_tables(
        context_lengths, new_units, old_pages, pages_dev
    )
    positions = (
        context_lengths[:, None] + jnp.arange(2, dtype=jnp.int32)[None, :]
    ).reshape(rows).astype(jnp.float32)
    half = HD // 2
    frequency = rope_base ** (-(jnp.arange(half, dtype=jnp.float32) * 2.0 / HD))
    angles = positions[:, None] * frequency
    cosine, sine = jnp.cos(angles), jnp.sin(angles)
    cosine = jnp.concatenate([cosine, cosine], axis=-1)
    sine = jnp.concatenate([-sine, sine], axis=-1)

    buffers = [
        pltpu.VMEM(cache_pages.shape, jnp.bfloat16), dma((pages_dev,)), dma((pages_dev,)),
    ]
    outgoing = pl.pallas_call(
        sort_kernel,
        out_shape=jax.ShapeDtypeStruct(cache_pages.shape, jnp.bfloat16),
        in_specs=[smem, hbm],
        out_specs=hbm,
        scratch_shapes=buffers,
        name="sort_pages",
    )(send_order, cache_pages)
    tile = (2 * group_count, HD)
    arrived, mixed, fresh = pl.pallas_call(
        lambda *refs: layer_kernel(devices, capacity, *refs),
        out_shape=(
            jax.ShapeDtypeStruct(cache_pages.shape, jnp.bfloat16),
            jax.ShapeDtypeStruct((rows, out_weight.shape[0]), jnp.bfloat16),
            jax.ShapeDtypeStruct((U_DEV, 2, 2 * HD), jnp.float32),
        ),
        in_specs=[smem, vmem, vmem, vmem, hbm, hbm, hbm],
        out_specs=(hbm, vmem, vmem),
        scratch_shapes=[
            pltpu.VMEM((heads, HD, D), jnp.bfloat16),
            pltpu.VMEM((tiles, HD, HEADS * HD), jnp.bfloat16),
            pltpu.VMEM(cache_pages.shape, jnp.bfloat16),
            pltpu.VMEM((devices, heads, rows, HD), jnp.bfloat16),
            pltpu.VMEM((units * 2 * group_count, HD), jnp.float32),
            pltpu.VMEM((units,) + tile, jnp.bfloat16),
            pltpu.VMEM((KVH, rows, HD), jnp.bfloat16),
            pltpu.VMEM((KVH, rows, HD), jnp.bfloat16),
            pltpu.VMEM((devices // 2, 2, U_DEV + 1) + tile, jnp.bfloat16),
            pltpu.VMEM((devices // 2, 2, U_DEV + 1) + tile, jnp.bfloat16),
            pltpu.VMEM((U_DEV + 1,) + tile, jnp.bfloat16),
            pltpu.VMEM((U_DEV + 1,) + tile, jnp.bfloat16),
            pltpu.VMEM((units,) + tile, jnp.bfloat16),
            pltpu.VMEM((rows, HEADS * HD), jnp.bfloat16),
            dma((heads + 1 + tiles,)),
            dma((capacity, devices)), dma((capacity, devices)),
            dma((2, devices // 2)), dma((2, devices // 2)),
            dma((devices // 2,)), dma((devices // 2,)),
            dma((2, devices // 2)), dma((2, devices // 2)),
            dma(()),
        ],
        compiler_params=pltpu.CompilerParams(
            collective_id=0, has_side_effects=True, vmem_limit_bytes=48 << 20
        ),
        name="layer",
    )(table, hidden_states.reshape(rows, D), cosine, sine, qkv_weight, out_weight, outgoing)
    own_lengths = jnp.take(
        context_lengths,
        lax.dynamic_slice_in_dim(new_units, lax.axis_index("tp") * U_DEV, U_DEV) // KVH,
    )
    placed = pl.pallas_call(
        place_kernel,
        out_shape=jax.ShapeDtypeStruct(cache_pages.shape, jnp.bfloat16),
        in_specs=[smem, smem, hbm, vmem],
        out_specs=hbm,
        scratch_shapes=buffers,
        name="place_pages",
    )(arrives_at, own_lengths, arrived, fresh)
    return (mixed.reshape(requests, 2, out_weight.shape[0]), placed)


def body(hidden_states, qkv_weight, out_weight, cache_pages, context_lengths, new_units, old_pages):
    devices = lax.axis_size("tp")
    whole_heads = qkv_weight.shape[0] % HD == 0 and out_weight.shape[0] % HD == 0
    whole_shares = cache_pages.shape[0] % devices == 0 and devices % 4 == 0 and hidden_states.shape[0] == KVH
    chosen = fused_body if whole_heads and whole_shares else plain_body
    return chosen(
        hidden_states, qkv_weight, out_weight, cache_pages, context_lengths, new_units, old_pages
    )


def solution(mesh):
    in_specs = (
        P("group", None, None),
        P("tp", None),
        P("tp", None),
        P(("group", "tp"), None, None),
        P("group"),
        P("group"),
        P("group"),
    )
    out_specs = (P("group", None, "tp"), P(("group", "tp"), None, None))
    return jax.shard_map(body, mesh=mesh, in_specs=in_specs, out_specs=out_specs, check_vma=False)
```

```python
import math

import jax
import jax.numpy as jnp
from jax import lax
from jax.experimental import pallas as pl
from jax.experimental.pallas import tpu as pltpu
from jax.sharding import PartitionSpec as P

D = 8192
HEADS = 64
KVH = 8
HD = 128
U_DEV = 4
MAXCTX = 2048
PAGE = 128


rope_base = 10000.0


def rotate_positions(values, positions):
    half_dim = values.shape[-1] // 2
    frequency = rope_base ** (-(jnp.arange(half_dim, dtype=jnp.float32) * 2.0 / values.shape[-1]))
    angles = positions.astype(jnp.float32)[..., None] * frequency
    cosine = jnp.concatenate([jnp.cos(angles), jnp.cos(angles)], axis=-1)
    sine_table = jnp.concatenate([jnp.sin(angles), jnp.sin(angles)], axis=-1)
    turned = jnp.concatenate([-values[..., half_dim:], values[..., :half_dim]], axis=-1)
    return values * cosine + turned * sine_table


def prepare(unit_qkv, base_lengths):
    group_count = HEADS // KVH
    count_units = unit_qkv.shape[0]
    positions = base_lengths[:, None] + jnp.arange(2, dtype=jnp.int32)[None, :]
    widened = unit_qkv.astype(jnp.float32)
    queries = widened[..., : group_count * HD].reshape(count_units, 2, group_count, HD)
    queries = rotate_positions(queries, positions[:, :, None]).astype(jnp.bfloat16)
    new_keys = rotate_positions(
        widened[..., group_count * HD : (group_count + 1) * HD], positions
    ).astype(jnp.bfloat16)
    new_values = unit_qkv[..., (group_count + 1) * HD :]
    return (queries, new_keys, new_values)


def context_terms(context, queries, valid_count):
    score_scale = 1.0 / math.sqrt(HD)
    cached_keys = context[..., :HD]
    cached_values = context[..., HD:]
    scores = (
        jnp.einsum("psgd,ptd->psgt", queries, cached_keys, preferred_element_type=jnp.float32)
        * score_scale
    )
    visible = jnp.arange(context.shape[1], dtype=jnp.int32)[None, :] < valid_count[:, None]
    weights = jnp.where(visible[:, None, None, :], jnp.exp(scores), 0.0)
    totals = jnp.sum(weights, axis=-1)
    weighted = jnp.einsum(
        "psgt,ptd->psgd",
        weights.astype(jnp.bfloat16),
        cached_values,
        preferred_element_type=jnp.float32,
    )
    return (weighted, totals)


def own_terms(queries, new_keys, new_values):
    score_scale = 1.0 / math.sqrt(HD)
    scores = (
        jnp.einsum("usgd,ujd->usgj", queries, new_keys, preferred_element_type=jnp.float32)
        * score_scale
    )
    recent = jnp.arange(2, dtype=jnp.int32)[None, :] <= jnp.arange(2, dtype=jnp.int32)[:, None]
    weights = jnp.where(recent[None, :, None, :], jnp.exp(scores), 0.0)
    totals = jnp.sum(weights, axis=-1)
    weighted = jnp.einsum(
        "usgj,ujd->usgd",
        weights.astype(jnp.bfloat16),
        new_values,
        preferred_element_type=jnp.float32,
    )
    return (weighted, totals)


def plain_body(hidden_states, qkv_weight, out_weight, cache_pages, context_lengths, new_units, old_pages):
    devices = lax.axis_size("tp")
    device = lax.axis_index("tp")
    requests = hidden_states.shape[0]
    rows_dev = qkv_weight.shape[0]
    pages_dev, page_rows, page_width = cache_pages.shape
    group_count = HEADS // KVH
    unit_rows = (group_count + 2) * HD
    per_unit = MAXCTX // PAGE
    unit_slots = U_DEV
    capacity = max(1, pages_dev // devices)
    total_units = new_units.shape[0]
    total_pages = old_pages.shape[0]
    flat_rows = hidden_states.reshape(requests * 2, D)
    partial_qkv = lax.dot_general(
        flat_rows, qkv_weight, (((1,), (1,)), ((), ())), preferred_element_type=jnp.float32
    )
    partial_qkv = partial_qkv.astype(jnp.bfloat16).reshape(requests, 2, rows_dev)
    slot_index = (
        jnp.zeros((total_units,), jnp.int32)
        .at[new_units]
        .set(jnp.arange(total_units, dtype=jnp.int32))
    )
    own_units = lax.dynamic_slice_in_dim(new_units, device * unit_slots, unit_slots)
    own_requests = own_units // KVH
    own_heads = own_units % KVH
    own_lengths = context_lengths[own_requests]
    local_ids = lax.dynamic_slice_in_dim(old_pages, device * pages_dev, pages_dev)
    local_units = local_ids // per_unit
    local_index = local_ids % per_unit
    target_dev = (slot_index[local_units] * per_unit + local_index) // pages_dev
    local_order = jnp.arange(pages_dev, dtype=jnp.int32)
    send_rank = jnp.sum(
        (
            (target_dev[:, None] == target_dev[None, :])
            & (local_order[None, :] < local_order[:, None])
        ).astype(jnp.int32),
        axis=1,
    )
    outgoing = (
        jnp.zeros((devices, capacity, page_rows, page_width), jnp.bfloat16)
        .at[target_dev, send_rank]
        .set(cache_pages)
    )
    arrived = lax.all_to_all(outgoing, "tp", split_axis=0, concat_axis=0, tiled=True)
    stored_position = (
        jnp.zeros((total_pages,), jnp.int32)
        .at[old_pages]
        .set(jnp.arange(total_pages, dtype=jnp.int32))
    )
    wanted = (
        own_units[:, None] * per_unit + jnp.arange(per_unit, dtype=jnp.int32)[None, :]
    ).reshape(pages_dev)
    source_pos = stored_position[wanted]
    source_dev = source_pos // pages_dev
    source_slot = source_pos % pages_dev
    arrival_rank = jnp.sum(
        (
            (source_dev[:, None] == source_dev[None, :])
            & (source_slot[None, :] < source_slot[:, None])
        ).astype(jnp.int32),
        axis=1,
    )
    relaid = arrived[source_dev, arrival_rank]
    contexts = relaid.reshape(unit_slots, MAXCTX, page_width)
    sources_per_head = unit_rows // rows_dev
    request_table = (new_units // KVH).reshape(devices, unit_slots)
    outgoing_rows = partial_qkv[request_table]
    incoming = lax.all_to_all(outgoing_rows, "tp", split_axis=0, concat_axis=0, tiled=True)
    grouped = jnp.moveaxis(incoming.reshape(KVH, sources_per_head, unit_slots, 2, rows_dev), 2, 0)
    chosen = jnp.take_along_axis(grouped, own_heads[:, None, None, None, None], axis=1)[:, 0]
    own_rows = chosen.transpose(0, 2, 1, 3).reshape(unit_slots, 2, unit_rows)
    queries, new_keys, new_values = prepare(own_rows, own_lengths)
    cache_sums, cache_totals = context_terms(contexts, queries, own_lengths)
    own_sums, own_totals = own_terms(queries, new_keys, new_values)
    attended = ((cache_sums + own_sums) / (cache_totals + own_totals)[..., None]).astype(
        jnp.bfloat16
    )
    attended = attended.reshape(unit_slots, 2, group_count * HD)
    all_heads = lax.all_gather(attended, "tp", axis=0, tiled=True)
    logical = (
        all_heads[slot_index]
        .reshape(requests, KVH, 2, group_count * HD)
        .transpose(0, 2, 1, 3)
        .reshape(requests * 2, HEADS * HD)
    )
    mixed_rows = lax.dot_general(
        logical, out_weight, (((1,), (1,)), ((), ())), preferred_element_type=jnp.float32
    )
    mixed_rows = mixed_rows.astype(jnp.bfloat16).reshape(requests, 2, out_weight.shape[0])
    fresh_rows = jnp.concatenate([new_keys, new_values], axis=-1)
    positions = jnp.arange(MAXCTX, dtype=jnp.int32)[None, :]
    contexts = jnp.where(
        (positions == own_lengths[:, None])[..., None], fresh_rows[:, 0:1], contexts
    )
    contexts = jnp.where(
        (positions == own_lengths[:, None] + 1)[..., None], fresh_rows[:, 1:2], contexts
    )
    return (mixed_rows, contexts.reshape(pages_dev, page_rows, page_width))


def index_tables(context_lengths, new_units, old_pages, pages_dev):
    device = lax.axis_index("tp")
    per_unit = MAXCTX // PAGE
    total_units = new_units.shape[0]
    total_pages = old_pages.shape[0]
    capacity = pages_dev // lax.axis_size("tp")
    places = jnp.arange(pages_dev, dtype=jnp.int32)
    slots = jnp.arange(total_units, dtype=jnp.int32)

    def pick(hit, values):
        return jnp.sum(jnp.where(hit, values[None, :], 0), axis=1)

    def ranks(owner, order):
        before = (owner[:, None] == owner[None, :]) & (order[None, :] < order[:, None])
        return jnp.sum(before.astype(jnp.int32), axis=1)

    local_ids = lax.dynamic_slice_in_dim(old_pages, device * pages_dev, pages_dev)
    target_slot = pick((local_ids // per_unit)[:, None] == new_units[None, :], slots)
    target_dev = target_slot // U_DEV
    sent_at = target_dev * capacity + ranks(target_dev, places)
    sent = places[:, None] == sent_at[None, :]
    send_order = pick(sent, places)
    send_ids = pick(sent, local_ids)
    send_slot = pick(sent, target_slot % U_DEV)
    own_units = lax.dynamic_slice_in_dim(new_units, device * U_DEV, U_DEV)
    wanted = (
        own_units[:, None] * per_unit + jnp.arange(per_unit, dtype=jnp.int32)[None, :]
    ).reshape(pages_dev)
    source_pos = pick(
        wanted[:, None] == old_pages[None, :], jnp.arange(total_pages, dtype=jnp.int32)
    )
    source_dev = source_pos // pages_dev
    arrives_at = source_dev * capacity + ranks(source_dev, source_pos)
    slot_of_unit = pick(slots[:, None] == new_units[None, :], slots)
    requests = context_lengths.shape[0]
    send_units = send_ids // per_unit
    send_lengths = pick(
        (send_units // KVH)[:, None] == jnp.arange(requests, dtype=jnp.int32)[None, :],
        context_lengths,
    )
    send_left = send_lengths - (send_ids % per_unit) * PAGE
    send_query = (send_units % KVH) * requests + send_units // KVH
    own_lengths = pick(
        (own_units // KVH)[:, None] == jnp.arange(requests, dtype=jnp.int32)[None, :],
        context_lengths,
    )
    own_heads, own_requests = own_units % KVH, own_units // KVH
    table = jnp.concatenate(
        [
            send_query, send_left, send_slot, slot_of_unit,
            own_heads * requests + own_requests, own_heads, own_requests,
        ]
    )
    return send_order, arrives_at, own_lengths, table


def sort_kernel(order_ref, pages_ref, out_ref, sem):
    count = out_ref.shape[0]

    def move(i):
        return pltpu.make_async_copy(pages_ref.at[order_ref[i]], out_ref.at[i], sem.at[i])

    @pl.loop(0, count)
    def _(i):
        move(i).start()

    @pl.loop(0, count)
    def _(i):
        move(i).wait()


def place_kernel(arrives_ref, lengths_ref, arrived_ref, fresh_ref, out_ref, buf, in_sem, out_sem):
    count = buf.shape[0]
    per_unit = MAXCTX // PAGE

    def inward(i):
        return pltpu.make_async_copy(arrived_ref.at[arrives_ref[i]], buf.at[i], in_sem.at[i])

    def outward(i):
        return pltpu.make_async_copy(buf.at[i], out_ref.at[i], out_sem.at[i])

    @pl.loop(0, count)
    def _(i):
        inward(i).start()

    @pl.loop(0, count)
    def _(i):
        inward(i).wait()
        slot = i // per_unit
        for step in range(2):
            position = lengths_ref[slot] + step

            @pl.when(position // PAGE == i % per_unit)
            def _():
                row = position % PAGE
                base = pl.multiple_of((row // 16) * 16, 16)
                tile = buf[i, pl.ds(base, 16), :]
                line = lax.broadcasted_iota(jnp.int32, tile.shape, 0)
                new = jnp.broadcast_to(fresh_ref[slot, step : step + 1, :], tile.shape)
                mixed = jnp.where(line == row - base, new, tile.astype(jnp.float32))
                buf[i, pl.ds(base, 16), :] = mixed.astype(jnp.bfloat16)

        outward(i).start()

    @pl.loop(0, count)
    def _(i):
        outward(i).wait()


NT = (((1,), (1,)), ((), ()))


def layer_kernel(
    devices, capacity,
    table, hidden_ref, cos_ref, sin_ref, qkv_hbm, out_hbm, pages_hbm,
    arrived_hbm, mixed_ref, fresh_ref,
    qkv_w, out_w, pages, rows_all, spread, queries, new_keys, new_values, part_out, part_in, swap_out, swap_in, att_all, flat,
    load_sem, page_send, page_recv, row_send, row_recv, part_send, part_recv, att_send, att_recv,
    self_sem,
):
    me = lax.axis_index("tp")
    pages_dev = pages.shape[0]
    rows = hidden_ref.shape[0]
    requests = rows // 2
    units = requests * KVH
    heads = qkv_w.shape[0]
    tiles = out_w.shape[0]
    group_count = HEADS // KVH
    head_rows = group_count + 2
    score_scale = 1.0 / math.sqrt(HD)
    span = requests * 2 * group_count
    at_left, at_target, at_slot = pages_dev, 2 * pages_dev, 3 * pages_dev
    at_own = at_slot + units
    at_head, at_request = at_own + U_DEV, at_own + 2 * U_DEV

    half = devices // 2
    here, side = lax.rem(me, half), me // half
    partner = lax.rem(me + half, devices)

    def near(offset):
        return side * half + lax.rem(here + offset, half)

    def near_sender(offset):
        return side * half + lax.rem(here + half - offset, half)

    def far(offset):
        return (1 - side) * half + lax.rem(here + offset, half)

    def far_sender(offset):
        return (1 - side) * half + lax.rem(here + half - offset, half)

    def remote(src, dst, send, recv, device):
        return pltpu.make_async_remote_copy(
            src_ref=src, dst_ref=dst, send_sem=send, recv_sem=recv,
            device_id={"tp": device}, device_id_type=pl.DeviceIdType.MESH,
        )

    def page_copy(rank, place, device):
        return remote(
            pages_hbm.at[device * capacity + rank], arrived_hbm.at[me * capacity + rank],
            page_send.at[rank, place], page_recv.at[rank, place], device,
        )

    def page_arrival(rank, place, device):
        at = device * capacity + rank
        return remote(
            pages_hbm.at[at], arrived_hbm.at[at],
            page_send.at[rank, place], page_recv.at[rank, place], device,
        )

    def row_copy(stage, place, owner, device):
        block = rows_all.at[owner]
        return remote(block, block, row_send.at[stage, place], row_recv.at[stage, place], device)

    def att_copy(stage, place, owner, device):
        block = att_all.at[pl.ds(owner * U_DEV, U_DEV)]
        return remote(block, block, att_send.at[stage, place], att_recv.at[stage, place], device)

    def part_copy(place, src, dst, device):
        return remote(
            part_out.at[src], part_in.at[dst], part_send.at[place], part_recv.at[place], device
        )

    def swap_copy():
        return remote(swap_out, swap_in, part_send.at[0], part_recv.at[0], partner)

    batches = 2 * capacity

    def send_pages(batch):
        if batch >= batches:
            return
        rank, low, high = batch // 2, (batch % 2) * (half // 2), (batch % 2 + 1) * (half // 2)
        if batch % 2:
            high = half

        if low == 0:
            page_copy(rank, 0, partner).start()

        @pl.loop(max(low, 1), high)
        def _(offset):
            page_copy(rank, offset, far(offset)).start()
            page_copy(rank, half + offset, near(offset)).start()

    def pack_totals(values):
        packed = jnp.zeros((2 * group_count, PAGE), jnp.float32)
        for j, total in enumerate(values):
            top = total.astype(jnp.bfloat16).astype(jnp.float32)
            packed = jnp.where(lane == j * strip, top, packed)
            packed = jnp.where(lane == j * strip + strip // 2, total - top, packed)
        return packed.astype(jnp.bfloat16)

    def unpack_total(packed, j):
        return jnp.sum(jnp.where(lane // strip == j, packed, 0.0), axis=-1, keepdims=True)

    lane = lax.broadcasted_iota(jnp.int32, (2 * group_count, PAGE), 1)
    strip = PAGE // U_DEV

    barrier = pltpu.get_barrier_semaphore()

    @pl.loop(1, devices)
    def _(offset):
        pl.semaphore_signal(
            barrier, inc=1, device_id={"tp": lax.rem(me + offset, devices)}, device_id_type=pl.DeviceIdType.MESH
        )

    loads = [
        pltpu.make_async_copy(qkv_hbm.at[pl.ds(c * HD, HD)], qkv_w.at[c], load_sem.at[c])
        for c in range(heads)
    ]
    loads.append(pltpu.make_async_copy(pages_hbm, pages, load_sem.at[heads]))
    loads += [
        pltpu.make_async_copy(
            out_hbm.at[pl.ds(c * HD, HD)], out_w.at[c], load_sem.at[heads + 1 + c]
        )
        for c in range(tiles)
    ]
    for load in loads[: heads + 1]:
        load.start()
    pl.semaphore_wait(barrier, devices - 1)
    send_pages(0)
    send_pages(1)

    for c in range(heads):
        loads[c].wait()
        part = lax.dot_general(
            hidden_ref[...], qkv_w[c], NT, preferred_element_type=jnp.float32
        ).astype(jnp.bfloat16).astype(jnp.float32)
        turned = part * cos_ref[...] + pltpu.roll(part, HD // 2, 1) * sin_ref[...]
        is_value = lax.rem(me * heads + c, head_rows) == head_rows - 1
        rows_all[me, c] = jnp.where(is_value, part, turned).astype(jnp.bfloat16)

    row_copy(0, 0, me, partner).start()

    @pl.loop(1, half)
    def _(offset):
        row_copy(0, offset, me, near(offset)).start()

    send_pages(2)
    for load in loads[heads + 1 :]:
        load.start()
    loads[heads].wait()
    own_pages = pltpu.make_async_copy(
        pages.at[pl.ds(me * capacity, capacity)],
        arrived_hbm.at[pl.ds(me * capacity, capacity)],
        self_sem,
    )
    own_pages.start()

    row_copy(0, 0, partner, partner).wait_recv()

    @pl.loop(1, half)
    def _(offset):
        row_copy(1, offset, partner, near(offset)).start()

    send_pages(3)

    @pl.loop(1, half)
    def _(offset):
        source = near_sender(offset)
        row_copy(0, offset, source, source).wait_recv()
        row_copy(1, offset, lax.rem(source + half, devices), source).wait_recv()

    for h in range(KVH):
        for g in range(group_count):
            at = h * head_rows + g
            spread[pl.ds(h * span + g, rows, stride=group_count), :] = rows_all[
                at // heads, at % heads
            ].astype(jnp.float32)
        at = h * head_rows + group_count
        new_keys[h] = rows_all[at // heads, at % heads]
        new_values[h] = rows_all[(at + 1) // heads, (at + 1) % heads]
        for r in range(requests):
            start = h * span + r * 2 * group_count
            queries[h * requests + r] = spread[start : start + 2 * group_count, :].astype(
                jnp.bfloat16
            )

    @pl.loop(0, devices)
    def _(target):
        zero = jnp.zeros((2 * group_count, PAGE), jnp.float32)
        sums, totals = [zero] * U_DEV, [zero[:, :1]] * U_DEV
        for rank in range(capacity):
            query = queries[table[target * capacity + rank]]
            left = table[at_left + target * capacity + rank]
            page = pages[target * capacity + rank]
            scores = lax.dot_general(
                query, page[:, :HD], NT, preferred_element_type=jnp.float32
            ) * score_scale
            weights = jnp.where(lane < left, jnp.exp(scores), 0.0)
            total = jnp.sum(weights, axis=-1, keepdims=True)
            weighted = jnp.dot(
                weights.astype(jnp.bfloat16), page[:, HD:], preferred_element_type=jnp.float32
            )
            slot = table[at_target + target * capacity + rank]
            for j in range(U_DEV):
                sums[j] = sums[j] + jnp.where(slot == j, weighted, 0.0)
                totals[j] = totals[j] + jnp.where(slot == j, total, 0.0)
        place, which = lax.rem(target, half), target // half
        for j in range(U_DEV):
            part_out[place, which, j] = sums[j].astype(jnp.bfloat16)
        part_out[place, which, U_DEV] = pack_totals(totals)

    @pl.loop(1, half)
    def _(offset):
        part_copy(offset, lax.rem(here + offset, half), here, near(offset)).start()

    send_pages(4)

    own_sums, own_totals = [], []
    row = lax.broadcasted_iota(jnp.int32, (2 * group_count, rows), 0)
    col = lax.broadcasted_iota(jnp.int32, (2 * group_count, rows), 1)
    line = lax.broadcasted_iota(jnp.int32, (rows, HD), 0)
    for j in range(U_DEV):
        request = table[at_request + j]
        keys = new_keys[table[at_head + j]]
        values = new_values[table[at_head + j]]
        scores = lax.dot_general(
            queries[table[at_own + j]], keys, NT, preferred_element_type=jnp.float32
        ) * score_scale
        seen = (col // 2 == request) & (col % 2 <= row // group_count)
        weights = jnp.where(seen, jnp.exp(scores), 0.0)
        own_totals.append(jnp.sum(weights, axis=-1, keepdims=True))
        own_sums.append(
            jnp.dot(weights.astype(jnp.bfloat16), values, preferred_element_type=jnp.float32)
        )
        for step in range(2):
            mine = line == request * 2 + step
            for part, kind in ((0, keys), (1, values)):
                fresh_ref[j, step : step + 1, part * HD : (part + 1) * HD] = jnp.sum(
                    jnp.where(mine, kind.astype(jnp.float32), 0.0), axis=0, keepdims=True
                )

    @pl.loop(1, half)
    def _(offset):
        source = near_sender(offset)
        part_copy(offset, here, lax.rem(here + half - offset, half), source).wait_recv()

    def half_sum(which):
        def add(offset, carry):
            block = part_in.at[lax.rem(here + offset, half), which]
            return tuple(c + block[j].astype(jnp.float32) for j, c in enumerate(carry))

        first = tuple(
            part_out[here, which, j].astype(jnp.float32) for j in range(U_DEV + 1)
        )
        return lax.fori_loop(1, half, add, first)

    away = half_sum(1 - side)
    for j in range(U_DEV):
        swap_out[j] = away[j].astype(jnp.bfloat16)
    swap_out[U_DEV] = pack_totals([unpack_total(away[U_DEV], j) for j in range(U_DEV)])
    kept = half_sum(side)
    swap_copy().start()
    send_pages(5)
    swap_copy().wait_recv()
    packed = kept[U_DEV] + swap_in[U_DEV].astype(jnp.float32)
    for j in range(U_DEV):
        total = own_totals[j] + unpack_total(packed, j)
        weighted = own_sums[j] + kept[j] + swap_in[j].astype(jnp.float32)
        att_all[me * U_DEV + j] = (weighted / total).astype(jnp.bfloat16)

    att_copy(0, 0, me, partner).start()

    @pl.loop(1, half)
    def _(offset):
        att_copy(0, offset, me, near(offset)).start()

    send_pages(6)
    att_copy(0, 0, partner, partner).wait_recv()

    @pl.loop(1, half)
    def _(offset):
        att_copy(1, offset, partner, near(offset)).start()

    for batch in range(7, batches):
        send_pages(batch)

    @pl.loop(1, half)
    def _(offset):
        source = near_sender(offset)
        att_copy(0, offset, source, source).wait_recv()
        att_copy(1, offset, lax.rem(source + half, devices), source).wait_recv()

    for r in range(requests):
        for h in range(KVH):
            slot = table[at_slot + r * KVH + h]
            spread[h * span + r * 2 * group_count : h * span + (r + 1) * 2 * group_count, :] = (
                att_all[slot].astype(jnp.float32)
            )
    for h in range(KVH):
        for g in range(group_count):
            at = (h * group_count + g) * HD
            flat[:, at : at + HD] = spread[
                pl.ds(h * span + g, rows, stride=group_count), :
            ].astype(jnp.bfloat16)
    for c in range(tiles):
        loads[heads + 1 + c].wait()
        mixed_ref[:, c * HD : (c + 1) * HD] = lax.dot_general(
            flat[...], out_w[c], NT, preferred_element_type=jnp.float32
        ).astype(jnp.bfloat16)

    own_pages.wait()

    row_copy(0, 0, me, partner).wait_send()
    att_copy(0, 0, me, partner).wait_send()
    swap_copy().wait_send()

    @pl.loop(1, half)
    def _(offset):
        for stage, owner in ((0, me), (1, partner)):
            row_copy(stage, offset, owner, near(offset)).wait_send()
            att_copy(stage, offset, owner, near(offset)).wait_send()
        part_copy(offset, lax.rem(here + offset, half), here, near(offset)).wait_send()

    for rank in range(capacity):
        page_copy(rank, 0, partner).wait_send()
        page_arrival(rank, 0, partner).wait_recv()

        @pl.loop(1, half)
        def _(offset):
            page_copy(rank, offset, far(offset)).wait_send()
            page_arrival(rank, offset, far_sender(offset)).wait_recv()
            page_copy(rank, half + offset, near(offset)).wait_send()
            page_arrival(rank, half + offset, near_sender(offset)).wait_recv()


def fused_body(hidden_states, qkv_weight, out_weight, cache_pages, context_lengths, new_units, old_pages):
    devices = lax.axis_size("tp")
    requests = hidden_states.shape[0]
    rows = requests * 2
    pages_dev = cache_pages.shape[0]
    capacity = pages_dev // devices
    heads = qkv_weight.shape[0] // HD
    tiles = out_weight.shape[0] // HD
    group_count = HEADS // KVH
    units = new_units.shape[0]
    hbm = pl.BlockSpec(memory_space=pl.ANY)
    vmem = pl.BlockSpec(memory_space=pltpu.VMEM)
    smem = pl.BlockSpec(memory_space=pltpu.SMEM)
    dma = pltpu.SemaphoreType.DMA
    send_order, arrives_at, own_lengths, table = index_tables(
        context_lengths, new_units, old_pages, pages_dev
    )
    positions = (
        context_lengths[:, None] + jnp.arange(2, dtype=jnp.int32)[None, :]
    ).reshape(rows).astype(jnp.float32)
    half = HD // 2
    frequency = rope_base ** (-(jnp.arange(half, dtype=jnp.float32) * 2.0 / HD))
    angles = positions[:, None] * frequency
    cosine, sine = jnp.cos(angles), jnp.sin(angles)
    cosine = jnp.concatenate([cosine, cosine], axis=-1)
    sine = jnp.concatenate([-sine, sine], axis=-1)

    small_limit = 2 * cache_pages.size * cache_pages.dtype.itemsize
    buffers = [
        pltpu.VMEM(cache_pages.shape, jnp.bfloat16), dma((pages_dev,)), dma((pages_dev,)),
    ]
    outgoing = pl.pallas_call(
        sort_kernel,
        out_shape=jax.ShapeDtypeStruct(cache_pages.shape, jnp.bfloat16),
        in_specs=[smem, hbm],
        out_specs=vmem,
        scratch_shapes=[dma((pages_dev,))],
        compiler_params=pltpu.CompilerParams(vmem_limit_bytes=small_limit),
        name="sort_pages",
    )(send_order, cache_pages)
    tile = (2 * group_count, HD)
    arrived, mixed, fresh = pl.pallas_call(
        lambda *refs: layer_kernel(devices, capacity, *refs),
        out_shape=(
            jax.ShapeDtypeStruct(cache_pages.shape, jnp.bfloat16),
            jax.ShapeDtypeStruct((rows, out_weight.shape[0]), jnp.bfloat16),
            jax.ShapeDtypeStruct((U_DEV, 2, 2 * HD), jnp.float32),
        ),
        in_specs=[smem, vmem, vmem, vmem, hbm, hbm, hbm],
        out_specs=(hbm, vmem, vmem),
        scratch_shapes=[
            pltpu.VMEM((heads, HD, D), jnp.bfloat16),
            pltpu.VMEM((tiles, HD, HEADS * HD), jnp.bfloat16),
            pltpu.VMEM(cache_pages.shape, jnp.bfloat16),
            pltpu.VMEM((devices, heads, rows, HD), jnp.bfloat16),
            pltpu.VMEM((units * 2 * group_count, HD), jnp.float32),
            pltpu.VMEM((units,) + tile, jnp.bfloat16),
            pltpu.VMEM((KVH, rows, HD), jnp.bfloat16),
            pltpu.VMEM((KVH, rows, HD), jnp.bfloat16),
            pltpu.VMEM((devices // 2, 2, U_DEV + 1) + tile, jnp.bfloat16),
            pltpu.VMEM((devices // 2, 2, U_DEV + 1) + tile, jnp.bfloat16),
            pltpu.VMEM((U_DEV + 1,) + tile, jnp.bfloat16),
            pltpu.VMEM((U_DEV + 1,) + tile, jnp.bfloat16),
            pltpu.VMEM((units,) + tile, jnp.bfloat16),
            pltpu.VMEM((rows, HEADS * HD), jnp.bfloat16),
            dma((heads + 1 + tiles,)),
            dma((capacity, devices)), dma((capacity, devices)),
            dma((2, devices // 2)), dma((2, devices // 2)),
            dma((devices // 2,)), dma((devices // 2,)),
            dma((2, devices // 2)), dma((2, devices // 2)),
            dma(()),
        ],
        compiler_params=pltpu.CompilerParams(
            collective_id=0, has_side_effects=True, vmem_limit_bytes=48 << 20
        ),
        name="layer",
    )(table, hidden_states.reshape(rows, D), cosine, sine, qkv_weight, out_weight, outgoing)
    placed = pl.pallas_call(
        place_kernel,
        out_shape=jax.ShapeDtypeStruct(cache_pages.shape, jnp.bfloat16),
        in_specs=[smem, smem, hbm, vmem],
        out_specs=hbm,
        scratch_shapes=buffers,
        compiler_params=pltpu.CompilerParams(vmem_limit_bytes=small_limit),
        name="place_pages",
    )(arrives_at, own_lengths, arrived, fresh)
    return (mixed.reshape(requests, 2, out_weight.shape[0]), placed)


def body(hidden_states, qkv_weight, out_weight, cache_pages, context_lengths, new_units, old_pages):
    devices = lax.axis_size("tp")
    whole_heads = qkv_weight.shape[0] % HD == 0 and out_weight.shape[0] % HD == 0
    whole_shares = cache_pages.shape[0] % devices == 0 and devices % 4 == 0 and hidden_states.shape[0] == KVH
    chosen = fused_body if whole_heads and whole_shares else plain_body
    return chosen(
        hidden_states, qkv_weight, out_weight, cache_pages, context_lengths, new_units, old_pages
    )


def solution(mesh):
    in_specs = (
        P("group", None, None),
        P("tp", None),
        P("tp", None),
        P(("group", "tp"), None, None),
        P("group"),
        P("group"),
        P("group"),
    )
    out_specs = (P("group", None, "tp"), P(("group", "tp"), None, None))
    return jax.shard_map(body, mesh=mesh, in_specs=in_specs, out_specs=out_specs, check_vma=False)
```

```python
import math

import jax
import jax.numpy as jnp
from jax import lax
from jax.experimental import pallas as pl
from jax.experimental.pallas import tpu as pltpu
from jax.sharding import PartitionSpec as P

D = 8192
HEADS = 64
KVH = 8
HD = 128
U_DEV = 4
MAXCTX = 2048
PAGE = 128


rope_base = 10000.0


def rotate_positions(values, positions):
    half_dim = values.shape[-1] // 2
    frequency = rope_base ** (-(jnp.arange(half_dim, dtype=jnp.float32) * 2.0 / values.shape[-1]))
    angles = positions.astype(jnp.float32)[..., None] * frequency
    cosine = jnp.concatenate([jnp.cos(angles), jnp.cos(angles)], axis=-1)
    sine_table = jnp.concatenate([jnp.sin(angles), jnp.sin(angles)], axis=-1)
    turned = jnp.concatenate([-values[..., half_dim:], values[..., :half_dim]], axis=-1)
    return values * cosine + turned * sine_table


def prepare(unit_qkv, base_lengths):
    group_count = HEADS // KVH
    count_units = unit_qkv.shape[0]
    positions = base_lengths[:, None] + jnp.arange(2, dtype=jnp.int32)[None, :]
    widened = unit_qkv.astype(jnp.float32)
    queries = widened[..., : group_count * HD].reshape(count_units, 2, group_count, HD)
    queries = rotate_positions(queries, positions[:, :, None]).astype(jnp.bfloat16)
    new_keys = rotate_positions(
        widened[..., group_count * HD : (group_count + 1) * HD], positions
    ).astype(jnp.bfloat16)
    new_values = unit_qkv[..., (group_count + 1) * HD :]
    return (queries, new_keys, new_values)


def context_terms(context, queries, valid_count):
    score_scale = 1.0 / math.sqrt(HD)
    cached_keys = context[..., :HD]
    cached_values = context[..., HD:]
    scores = (
        jnp.einsum("psgd,ptd->psgt", queries, cached_keys, preferred_element_type=jnp.float32)
        * score_scale
    )
    visible = jnp.arange(context.shape[1], dtype=jnp.int32)[None, :] < valid_count[:, None]
    weights = jnp.where(visible[:, None, None, :], jnp.exp(scores), 0.0)
    totals = jnp.sum(weights, axis=-1)
    weighted = jnp.einsum(
        "psgt,ptd->psgd",
        weights.astype(jnp.bfloat16),
        cached_values,
        preferred_element_type=jnp.float32,
    )
    return (weighted, totals)


def own_terms(queries, new_keys, new_values):
    score_scale = 1.0 / math.sqrt(HD)
    scores = (
        jnp.einsum("usgd,ujd->usgj", queries, new_keys, preferred_element_type=jnp.float32)
        * score_scale
    )
    recent = jnp.arange(2, dtype=jnp.int32)[None, :] <= jnp.arange(2, dtype=jnp.int32)[:, None]
    weights = jnp.where(recent[None, :, None, :], jnp.exp(scores), 0.0)
    totals = jnp.sum(weights, axis=-1)
    weighted = jnp.einsum(
        "usgj,ujd->usgd",
        weights.astype(jnp.bfloat16),
        new_values,
        preferred_element_type=jnp.float32,
    )
    return (weighted, totals)


def plain_body(hidden_states, qkv_weight, out_weight, cache_pages, context_lengths, new_units, old_pages):
    devices = lax.axis_size("tp")
    device = lax.axis_index("tp")
    requests = hidden_states.shape[0]
    rows_dev = qkv_weight.shape[0]
    pages_dev, page_rows, page_width = cache_pages.shape
    group_count = HEADS // KVH
    unit_rows = (group_count + 2) * HD
    per_unit = MAXCTX // PAGE
    unit_slots = U_DEV
    capacity = max(1, pages_dev // devices)
    total_units = new_units.shape[0]
    total_pages = old_pages.shape[0]
    flat_rows = hidden_states.reshape(requests * 2, D)
    partial_qkv = lax.dot_general(
        flat_rows, qkv_weight, (((1,), (1,)), ((), ())), preferred_element_type=jnp.float32
    )
    partial_qkv = partial_qkv.astype(jnp.bfloat16).reshape(requests, 2, rows_dev)
    slot_index = (
        jnp.zeros((total_units,), jnp.int32)
        .at[new_units]
        .set(jnp.arange(total_units, dtype=jnp.int32))
    )
    own_units = lax.dynamic_slice_in_dim(new_units, device * unit_slots, unit_slots)
    own_requests = own_units // KVH
    own_heads = own_units % KVH
    own_lengths = context_lengths[own_requests]
    local_ids = lax.dynamic_slice_in_dim(old_pages, device * pages_dev, pages_dev)
    local_units = local_ids // per_unit
    local_index = local_ids % per_unit
    target_dev = (slot_index[local_units] * per_unit + local_index) // pages_dev
    local_order = jnp.arange(pages_dev, dtype=jnp.int32)
    send_rank = jnp.sum(
        (
            (target_dev[:, None] == target_dev[None, :])
            & (local_order[None, :] < local_order[:, None])
        ).astype(jnp.int32),
        axis=1,
    )
    outgoing = (
        jnp.zeros((devices, capacity, page_rows, page_width), jnp.bfloat16)
        .at[target_dev, send_rank]
        .set(cache_pages)
    )
    arrived = lax.all_to_all(outgoing, "tp", split_axis=0, concat_axis=0, tiled=True)
    stored_position = (
        jnp.zeros((total_pages,), jnp.int32)
        .at[old_pages]
        .set(jnp.arange(total_pages, dtype=jnp.int32))
    )
    wanted = (
        own_units[:, None] * per_unit + jnp.arange(per_unit, dtype=jnp.int32)[None, :]
    ).reshape(pages_dev)
    source_pos = stored_position[wanted]
    source_dev = source_pos // pages_dev
    source_slot = source_pos % pages_dev
    arrival_rank = jnp.sum(
        (
            (source_dev[:, None] == source_dev[None, :])
            & (source_slot[None, :] < source_slot[:, None])
        ).astype(jnp.int32),
        axis=1,
    )
    relaid = arrived[source_dev, arrival_rank]
    contexts = relaid.reshape(unit_slots, MAXCTX, page_width)
    sources_per_head = unit_rows // rows_dev
    request_table = (new_units // KVH).reshape(devices, unit_slots)
    outgoing_rows = partial_qkv[request_table]
    incoming = lax.all_to_all(outgoing_rows, "tp", split_axis=0, concat_axis=0, tiled=True)
    grouped = jnp.moveaxis(incoming.reshape(KVH, sources_per_head, unit_slots, 2, rows_dev), 2, 0)
    chosen = jnp.take_along_axis(grouped, own_heads[:, None, None, None, None], axis=1)[:, 0]
    own_rows = chosen.transpose(0, 2, 1, 3).reshape(unit_slots, 2, unit_rows)
    queries, new_keys, new_values = prepare(own_rows, own_lengths)
    cache_sums, cache_totals = context_terms(contexts, queries, own_lengths)
    own_sums, own_totals = own_terms(queries, new_keys, new_values)
    attended = ((cache_sums + own_sums) / (cache_totals + own_totals)[..., None]).astype(
        jnp.bfloat16
    )
    attended = attended.reshape(unit_slots, 2, group_count * HD)
    all_heads = lax.all_gather(attended, "tp", axis=0, tiled=True)
    logical = (
        all_heads[slot_index]
        .reshape(requests, KVH, 2, group_count * HD)
        .transpose(0, 2, 1, 3)
        .reshape(requests * 2, HEADS * HD)
    )
    mixed_rows = lax.dot_general(
        logical, out_weight, (((1,), (1,)), ((), ())), preferred_element_type=jnp.float32
    )
    mixed_rows = mixed_rows.astype(jnp.bfloat16).reshape(requests, 2, out_weight.shape[0])
    fresh_rows = jnp.concatenate([new_keys, new_values], axis=-1)
    positions = jnp.arange(MAXCTX, dtype=jnp.int32)[None, :]
    contexts = jnp.where(
        (positions == own_lengths[:, None])[..., None], fresh_rows[:, 0:1], contexts
    )
    contexts = jnp.where(
        (positions == own_lengths[:, None] + 1)[..., None], fresh_rows[:, 1:2], contexts
    )
    return (mixed_rows, contexts.reshape(pages_dev, page_rows, page_width))


def index_tables(context_lengths, new_units, old_pages, pages_dev):
    device = lax.axis_index("tp")
    per_unit = MAXCTX // PAGE
    total_units = new_units.shape[0]
    total_pages = old_pages.shape[0]
    capacity = pages_dev // lax.axis_size("tp")
    places = jnp.arange(pages_dev, dtype=jnp.int32)
    slots = jnp.arange(total_units, dtype=jnp.int32)

    def pick(hit, values):
        return jnp.sum(jnp.where(hit, values[None, :], 0), axis=1)

    def ranks(owner, order):
        before = (owner[:, None] == owner[None, :]) & (order[None, :] < order[:, None])
        return jnp.sum(before.astype(jnp.int32), axis=1)

    local_ids = lax.dynamic_slice_in_dim(old_pages, device * pages_dev, pages_dev)
    target_slot = pick((local_ids // per_unit)[:, None] == new_units[None, :], slots)
    target_dev = target_slot // U_DEV
    sent_at = target_dev * capacity + ranks(target_dev, places)
    sent = places[:, None] == sent_at[None, :]
    send_order = pick(sent, places)
    send_ids = pick(sent, local_ids)
    send_slot = pick(sent, target_slot % U_DEV)
    own_units = lax.dynamic_slice_in_dim(new_units, device * U_DEV, U_DEV)
    wanted = (
        own_units[:, None] * per_unit + jnp.arange(per_unit, dtype=jnp.int32)[None, :]
    ).reshape(pages_dev)
    source_pos = pick(
        wanted[:, None] == old_pages[None, :], jnp.arange(total_pages, dtype=jnp.int32)
    )
    source_dev = source_pos // pages_dev
    arrives_at = source_dev * capacity + ranks(source_dev, source_pos)
    slot_of_unit = pick(slots[:, None] == new_units[None, :], slots)
    requests = context_lengths.shape[0]
    send_units = send_ids // per_unit
    send_lengths = pick(
        (send_units // KVH)[:, None] == jnp.arange(requests, dtype=jnp.int32)[None, :],
        context_lengths,
    )
    send_left = send_lengths - (send_ids % per_unit) * PAGE
    send_query = (send_units % KVH) * requests + send_units // KVH
    own_lengths = pick(
        (own_units // KVH)[:, None] == jnp.arange(requests, dtype=jnp.int32)[None, :],
        context_lengths,
    )
    own_heads, own_requests = own_units % KVH, own_units // KVH
    table = jnp.concatenate(
        [
            send_query, send_left, send_slot, slot_of_unit,
            own_heads * requests + own_requests, own_heads, own_requests,
        ]
    )
    return send_order, arrives_at, own_lengths, table


def sort_kernel(order_ref, pages_ref, out_ref, buf, in_sem, out_sem):
    count = buf.shape[0]

    def inward(i):
        return pltpu.make_async_copy(pages_ref.at[order_ref[i]], buf.at[i], in_sem.at[i])

    def outward(i):
        return pltpu.make_async_copy(buf.at[i], out_ref.at[i], out_sem.at[i])

    @pl.loop(0, count)
    def _(i):
        inward(i).start()

    @pl.loop(0, count)
    def _(i):
        inward(i).wait()
        outward(i).start()

    @pl.loop(0, count)
    def _(i):
        outward(i).wait()


def place_kernel(arrives_ref, lengths_ref, arrived_ref, fresh_ref, out_ref, buf, in_sem, out_sem):
    count = buf.shape[0]
    per_unit = MAXCTX // PAGE

    def inward(i):
        return pltpu.make_async_copy(arrived_ref.at[arrives_ref[i]], buf.at[i], in_sem.at[i])

    def outward(i):
        return pltpu.make_async_copy(buf.at[i], out_ref.at[i], out_sem.at[i])

    @pl.loop(0, count)
    def _(i):
        inward(i).start()

    @pl.loop(0, count)
    def _(i):
        inward(i).wait()
        slot = i // per_unit
        for step in range(2):
            position = lengths_ref[slot] + step

            @pl.when(position // PAGE == i % per_unit)
            def _():
                row = position % PAGE
                base = pl.multiple_of((row // 16) * 16, 16)
                tile = buf[i, pl.ds(base, 16), :]
                line = lax.broadcasted_iota(jnp.int32, tile.shape, 0)
                new = jnp.broadcast_to(fresh_ref[slot, step : step + 1, :], tile.shape)
                mixed = jnp.where(line == row - base, new, tile.astype(jnp.float32))
                buf[i, pl.ds(base, 16), :] = mixed.astype(jnp.bfloat16)

        outward(i).start()

    @pl.loop(0, count)
    def _(i):
        outward(i).wait()


NT = (((1,), (1,)), ((), ()))


def layer_kernel(
    devices, capacity,
    table, hidden_ref, cos_ref, sin_ref, qkv_hbm, out_hbm, pages_hbm,
    arrived_hbm, mixed_ref, fresh_ref,
    qkv_w, out_w, pages, rows_all, spread, queries, new_keys, new_values, part_out, part_in, swap_out, swap_in, att_all, flat,
    load_sem, page_send, page_recv, row_send, row_recv, part_send, part_recv, att_send, att_recv,
    self_sem,
):
    me = lax.axis_index("tp")
    pages_dev = pages.shape[0]
    rows = hidden_ref.shape[0]
    requests = rows // 2
    units = requests * KVH
    heads = qkv_w.shape[0]
    tiles = out_w.shape[0]
    group_count = HEADS // KVH
    head_rows = group_count + 2
    score_scale = 1.0 / math.sqrt(HD)
    span = requests * 2 * group_count
    at_left, at_target, at_slot = pages_dev, 2 * pages_dev, 3 * pages_dev
    at_own = at_slot + units
    at_head, at_request = at_own + U_DEV, at_own + 2 * U_DEV

    half = devices // 2
    here, side = lax.rem(me, half), me // half
    partner = lax.rem(me + half, devices)

    def near(offset):
        return side * half + lax.rem(here + offset, half)

    def near_sender(offset):
        return side * half + lax.rem(here + half - offset, half)

    def far(offset):
        return (1 - side) * half + lax.rem(here + offset, half)

    def far_sender(offset):
        return (1 - side) * half + lax.rem(here + half - offset, half)

    def remote(src, dst, send, recv, device):
        return pltpu.make_async_remote_copy(
            src_ref=src, dst_ref=dst, send_sem=send, recv_sem=recv,
            device_id={"tp": device}, device_id_type=pl.DeviceIdType.MESH,
        )

    def page_copy(rank, place, device):
        return remote(
            pages_hbm.at[device * capacity + rank], arrived_hbm.at[me * capacity + rank],
            page_send.at[rank, place], page_recv.at[rank, place], device,
        )

    def page_arrival(rank, place, device):
        at = device * capacity + rank
        return remote(
            pages_hbm.at[at], arrived_hbm.at[at],
            page_send.at[rank, place], page_recv.at[rank, place], device,
        )

    def row_copy(stage, place, owner, device):
        block = rows_all.at[owner]
        return remote(block, block, row_send.at[stage, place], row_recv.at[stage, place], device)

    def att_copy(stage, place, owner, device):
        block = att_all.at[pl.ds(owner * U_DEV, U_DEV)]
        return remote(block, block, att_send.at[stage, place], att_recv.at[stage, place], device)

    def part_copy(place, src, dst, device):
        return remote(
            part_out.at[src], part_in.at[dst], part_send.at[place], part_recv.at[place], device
        )

    def swap_copy():
        return remote(swap_out, swap_in, part_send.at[0], part_recv.at[0], partner)

    batches = 2 * capacity

    def send_pages(batch):
        if batch >= batches:
            return
        rank, low, high = batch // 2, (batch % 2) * (half // 2), (batch % 2 + 1) * (half // 2)
        if batch % 2:
            high = half

        if low == 0:
            page_copy(rank, 0, partner).start()

        @pl.loop(max(low, 1), high)
        def _(offset):
            page_copy(rank, offset, far(offset)).start()
            page_copy(rank, half + offset, near(offset)).start()

    def pack_totals(values):
        packed = jnp.zeros((2 * group_count, PAGE), jnp.float32)
        for j, total in enumerate(values):
            top = total.astype(jnp.bfloat16).astype(jnp.float32)
            packed = jnp.where(lane == j * strip, top, packed)
            packed = jnp.where(lane == j * strip + strip // 2, total - top, packed)
        return packed.astype(jnp.bfloat16)

    def unpack_total(packed, j):
        return jnp.sum(jnp.where(lane // strip == j, packed, 0.0), axis=-1, keepdims=True)

    lane = lax.broadcasted_iota(jnp.int32, (2 * group_count, PAGE), 1)
    strip = PAGE // U_DEV

    barrier = pltpu.get_barrier_semaphore()

    @pl.loop(1, devices)
    def _(offset):
        pl.semaphore_signal(
            barrier, inc=1, device_id={"tp": lax.rem(me + offset, devices)}, device_id_type=pl.DeviceIdType.MESH
        )

    loads = [
        pltpu.make_async_copy(qkv_hbm.at[pl.ds(c * HD, HD)], qkv_w.at[c], load_sem.at[c])
        for c in range(heads)
    ]
    loads.append(pltpu.make_async_copy(pages_hbm, pages, load_sem.at[heads]))
    loads += [
        pltpu.make_async_copy(
            out_hbm.at[pl.ds(c * HD, HD)], out_w.at[c], load_sem.at[heads + 1 + c]
        )
        for c in range(tiles)
    ]
    for load in loads[: heads + 1]:
        load.start()
    pl.semaphore_wait(barrier, devices - 1)
    send_pages(0)
    send_pages(1)

    for c in range(heads):
        loads[c].wait()
        part = lax.dot_general(
            hidden_ref[...], qkv_w[c], NT, preferred_element_type=jnp.float32
        ).astype(jnp.bfloat16).astype(jnp.float32)
        turned = part * cos_ref[...] + pltpu.roll(part, HD // 2, 1) * sin_ref[...]
        is_value = lax.rem(me * heads + c, head_rows) == head_rows - 1
        rows_all[me, c] = jnp.where(is_value, part, turned).astype(jnp.bfloat16)

    row_copy(0, 0, me, partner).start()

    @pl.loop(1, half)
    def _(offset):
        row_copy(0, offset, me, near(offset)).start()

    send_pages(2)
    for load in loads[heads + 1 :]:
        load.start()
    loads[heads].wait()
    own_pages = pltpu.make_async_copy(
        pages.at[pl.ds(me * capacity, capacity)],
        arrived_hbm.at[pl.ds(me * capacity, capacity)],
        self_sem,
    )
    own_pages.start()

    row_copy(0, 0, partner, partner).wait_recv()

    @pl.loop(1, half)
    def _(offset):
        row_copy(1, offset, partner, near(offset)).start()

    send_pages(3)

    @pl.loop(1, half)
    def _(offset):
        source = near_sender(offset)
        row_copy(0, offset, source, source).wait_recv()
        row_copy(1, offset, lax.rem(source + half, devices), source).wait_recv()

    for h in range(KVH):
        for g in range(group_count):
            at = h * head_rows + g
            spread[pl.ds(h * span + g, rows, stride=group_count), :] = rows_all[
                at // heads, at % heads
            ].astype(jnp.float32)
        at = h * head_rows + group_count
        new_keys[h] = rows_all[at // heads, at % heads]
        new_values[h] = rows_all[(at + 1) // heads, (at + 1) % heads]
        for r in range(requests):
            start = h * span + r * 2 * group_count
            queries[h * requests + r] = spread[start : start + 2 * group_count, :].astype(
                jnp.bfloat16
            )

    @pl.loop(0, devices)
    def _(target):
        zero = jnp.zeros((2 * group_count, PAGE), jnp.float32)
        sums, totals = [zero] * U_DEV, [zero[:, :1]] * U_DEV
        for rank in range(capacity):
            query = queries[table[target * capacity + rank]]
            left = table[at_left + target * capacity + rank]
            page = pages[target * capacity + rank]
            scores = lax.dot_general(
                query, page[:, :HD], NT, preferred_element_type=jnp.float32
            ) * score_scale
            weights = jnp.where(lane < left, jnp.exp(scores), 0.0)
            total = jnp.sum(weights, axis=-1, keepdims=True)
            weighted = jnp.dot(
                weights.astype(jnp.bfloat16), page[:, HD:], preferred_element_type=jnp.float32
            )
            slot = table[at_target + target * capacity + rank]
            for j in range(U_DEV):
                sums[j] = sums[j] + jnp.where(slot == j, weighted, 0.0)
                totals[j] = totals[j] + jnp.where(slot == j, total, 0.0)
        place, which = lax.rem(target, half), target // half
        for j in range(U_DEV):
            part_out[place, which, j] = sums[j].astype(jnp.bfloat16)
        part_out[place, which, U_DEV] = pack_totals(totals)

    @pl.loop(1, half)
    def _(offset):
        part_copy(offset, lax.rem(here + offset, half), here, near(offset)).start()

    send_pages(4)

    own_sums, own_totals = [], []
    row = lax.broadcasted_iota(jnp.int32, (2 * group_count, rows), 0)
    col = lax.broadcasted_iota(jnp.int32, (2 * group_count, rows), 1)
    line = lax.broadcasted_iota(jnp.int32, (rows, HD), 0)
    for j in range(U_DEV):
        request = table[at_request + j]
        keys = new_keys[table[at_head + j]]
        values = new_values[table[at_head + j]]
        scores = lax.dot_general(
            queries[table[at_own + j]], keys, NT, preferred_element_type=jnp.float32
        ) * score_scale
        seen = (col // 2 == request) & (col % 2 <= row // group_count)
        weights = jnp.where(seen, jnp.exp(scores), 0.0)
        own_totals.append(jnp.sum(weights, axis=-1, keepdims=True))
        own_sums.append(
            jnp.dot(weights.astype(jnp.bfloat16), values, preferred_element_type=jnp.float32)
        )
        for step in range(2):
            mine = line == request * 2 + step
            for part, kind in ((0, keys), (1, values)):
                fresh_ref[j, step : step + 1, part * HD : (part + 1) * HD] = jnp.sum(
                    jnp.where(mine, kind.astype(jnp.float32), 0.0), axis=0, keepdims=True
                )

    @pl.loop(1, half)
    def _(offset):
        source = near_sender(offset)
        part_copy(offset, here, lax.rem(here + half - offset, half), source).wait_recv()

    def half_sum(which):
        def add(offset, carry):
            block = part_in.at[lax.rem(here + offset, half), which]
            return tuple(c + block[j].astype(jnp.float32) for j, c in enumerate(carry))

        first = tuple(
            part_out[here, which, j].astype(jnp.float32) for j in range(U_DEV + 1)
        )
        return lax.fori_loop(1, half, add, first)

    away = half_sum(1 - side)
    for j in range(U_DEV):
        swap_out[j] = away[j].astype(jnp.bfloat16)
    swap_out[U_DEV] = pack_totals([unpack_total(away[U_DEV], j) for j in range(U_DEV)])
    kept = half_sum(side)
    swap_copy().start()
    send_pages(5)
    swap_copy().wait_recv()
    packed = kept[U_DEV] + swap_in[U_DEV].astype(jnp.float32)
    for j in range(U_DEV):
        total = own_totals[j] + unpack_total(packed, j)
        weighted = own_sums[j] + kept[j] + swap_in[j].astype(jnp.float32)
        att_all[me * U_DEV + j] = (weighted / total).astype(jnp.bfloat16)

    att_copy(0, 0, me, partner).start()

    @pl.loop(1, half)
    def _(offset):
        att_copy(0, offset, me, near(offset)).start()

    send_pages(6)
    att_copy(0, 0, partner, partner).wait_recv()

    @pl.loop(1, half)
    def _(offset):
        att_copy(1, offset, partner, near(offset)).start()

    for batch in range(7, batches):
        send_pages(batch)

    @pl.loop(1, half)
    def _(offset):
        source = near_sender(offset)
        att_copy(0, offset, source, source).wait_recv()
        att_copy(1, offset, lax.rem(source + half, devices), source).wait_recv()

    for r in range(requests):
        for h in range(KVH):
            slot = table[at_slot + r * KVH + h]
            spread[h * span + r * 2 * group_count : h * span + (r + 1) * 2 * group_count, :] = (
                att_all[slot].astype(jnp.float32)
            )
    for h in range(KVH):
        for g in range(group_count):
            at = (h * group_count + g) * HD
            flat[:, at : at + HD] = spread[
                pl.ds(h * span + g, rows, stride=group_count), :
            ].astype(jnp.bfloat16)
    for c in range(tiles):
        loads[heads + 1 + c].wait()
        mixed_ref[:, c * HD : (c + 1) * HD] = lax.dot_general(
            flat[...], out_w[c], NT, preferred_element_type=jnp.float32
        ).astype(jnp.bfloat16)

    own_pages.wait()

    row_copy(0, 0, me, partner).wait_send()
    att_copy(0, 0, me, partner).wait_send()
    swap_copy().wait_send()

    @pl.loop(1, half)
    def _(offset):
        for stage, owner in ((0, me), (1, partner)):
            row_copy(stage, offset, owner, near(offset)).wait_send()
            att_copy(stage, offset, owner, near(offset)).wait_send()
        part_copy(offset, lax.rem(here + offset, half), here, near(offset)).wait_send()

    for rank in range(capacity):
        page_copy(rank, 0, partner).wait_send()
        page_arrival(rank, 0, partner).wait_recv()

        @pl.loop(1, half)
        def _(offset):
            page_copy(rank, offset, far(offset)).wait_send()
            page_arrival(rank, offset, far_sender(offset)).wait_recv()
            page_copy(rank, half + offset, near(offset)).wait_send()
            page_arrival(rank, half + offset, near_sender(offset)).wait_recv()


def fused_body(hidden_states, qkv_weight, out_weight, cache_pages, context_lengths, new_units, old_pages):
    devices = lax.axis_size("tp")
    requests = hidden_states.shape[0]
    rows = requests * 2
    pages_dev = cache_pages.shape[0]
    capacity = pages_dev // devices
    heads = qkv_weight.shape[0] // HD
    tiles = out_weight.shape[0] // HD
    group_count = HEADS // KVH
    units = new_units.shape[0]
    hbm = pl.BlockSpec(memory_space=pltpu.HBM)
    vmem = pl.BlockSpec(memory_space=pltpu.VMEM)
    smem = pl.BlockSpec(memory_space=pltpu.SMEM)
    dma = pltpu.SemaphoreType.DMA
    send_order, arrives_at, own_lengths, table = index_tables(
        context_lengths, new_units, old_pages, pages_dev
    )
    positions = (
        context_lengths[:, None] + jnp.arange(2, dtype=jnp.int32)[None, :]
    ).reshape(rows).astype(jnp.float32)
    half = HD // 2
    frequency = rope_base ** (-(jnp.arange(half, dtype=jnp.float32) * 2.0 / HD))
    angles = positions[:, None] * frequency
    cosine, sine = jnp.cos(angles), jnp.sin(angles)
    cosine = jnp.concatenate([cosine, cosine], axis=-1)
    sine = jnp.concatenate([-sine, sine], axis=-1)

    buffers = [
        pltpu.VMEM(cache_pages.shape, jnp.bfloat16), dma((pages_dev,)), dma((pages_dev,)),
    ]
    outgoing = pl.pallas_call(
        sort_kernel,
        out_shape=jax.ShapeDtypeStruct(cache_pages.shape, jnp.bfloat16),
        in_specs=[smem, hbm],
        out_specs=hbm,
        scratch_shapes=buffers,
        name="sort_pages",
    )(send_order, cache_pages)
    tile = (2 * group_count, HD)
    arrived, mixed, fresh = pl.pallas_call(
        lambda *refs: layer_kernel(devices, capacity, *refs),
        out_shape=(
            jax.ShapeDtypeStruct(cache_pages.shape, jnp.bfloat16),
            jax.ShapeDtypeStruct((rows, out_weight.shape[0]), jnp.bfloat16),
            jax.ShapeDtypeStruct((U_DEV, 2, 2 * HD), jnp.float32),
        ),
        in_specs=[smem, vmem, vmem, vmem, hbm, hbm, hbm],
        out_specs=(hbm, vmem, vmem),
        scratch_shapes=[
            pltpu.VMEM((heads, HD, D), jnp.bfloat16),
            pltpu.VMEM((tiles, HD, HEADS * HD), jnp.bfloat16),
            pltpu.VMEM(cache_pages.shape, jnp.bfloat16),
            pltpu.VMEM((devices, heads, rows, HD), jnp.bfloat16),
            pltpu.VMEM((units * 2 * group_count, HD), jnp.float32),
            pltpu.VMEM((units,) + tile, jnp.bfloat16),
            pltpu.VMEM((KVH, rows, HD), jnp.bfloat16),
            pltpu.VMEM((KVH, rows, HD), jnp.bfloat16),
            pltpu.VMEM((devices // 2, 2, U_DEV + 1) + tile, jnp.bfloat16),
            pltpu.VMEM((devices // 2, 2, U_DEV + 1) + tile, jnp.bfloat16),
            pltpu.VMEM((U_DEV + 1,) + tile, jnp.bfloat16),
            pltpu.VMEM((U_DEV + 1,) + tile, jnp.bfloat16),
            pltpu.VMEM((units,) + tile, jnp.bfloat16),
            pltpu.VMEM((rows, HEADS * HD), jnp.bfloat16),
            dma((heads + 1 + tiles,)),
            dma((capacity, devices)), dma((capacity, devices)),
            dma((2, devices // 2)), dma((2, devices // 2)),
            dma((devices // 2,)), dma((devices // 2,)),
            dma((2, devices // 2)), dma((2, devices // 2)),
            dma(()),
        ],
        compiler_params=pltpu.CompilerParams(
            collective_id=0, has_side_effects=True, vmem_limit_bytes=61 << 20
        ),
        name="layer",
    )(table, hidden_states.reshape(rows, D), cosine, sine, qkv_weight, out_weight, outgoing)
    placed = pl.pallas_call(
        place_kernel,
        out_shape=jax.ShapeDtypeStruct(cache_pages.shape, jnp.bfloat16),
        in_specs=[smem, smem, hbm, vmem],
        out_specs=hbm,
        scratch_shapes=buffers,
        name="place_pages",
    )(arrives_at, own_lengths, arrived, fresh)
    return (mixed.reshape(requests, 2, out_weight.shape[0]), placed)


def body(hidden_states, qkv_weight, out_weight, cache_pages, context_lengths, new_units, old_pages):
    devices = lax.axis_size("tp")
    whole_heads = qkv_weight.shape[0] % HD == 0 and out_weight.shape[0] % HD == 0
    whole_shares = cache_pages.shape[0] % devices == 0 and devices % 4 == 0 and hidden_states.shape[0] == KVH
    chosen = fused_body if whole_heads and whole_shares else plain_body
    return chosen(
        hidden_states, qkv_weight, out_weight, cache_pages, context_lengths, new_units, old_pages
    )


def solution(mesh):
    in_specs = (
        P("group", None, None),
        P("tp", None),
        P("tp", None),
        P(("group", "tp"), None, None),
        P("group"),
        P("group"),
        P("group"),
    )
    out_specs = (P("group", None, "tp"), P(("group", "tp"), None, None))
    return jax.shard_map(body, mesh=mesh, in_specs=in_specs, out_specs=out_specs, check_vma=False)
```
